32 devices in a mesh: ctx: 4 (over y, x), dp: 8 (over z, core).
Axes of the slice: x: 2, y: 2, z: 4, core: 2. Of those that a mesh axis runs over, the one named last changes fastest.
Arguments:
- queries: bfloat16 [8, 512, 1024], P('dp', 'ctx'), may hold values from -6 to 6
- keys_in: bfloat16 [8, 512, 256], P('dp', 'ctx'), may hold values from -6 to 6
- values_in: bfloat16 [8, 512, 256], P('dp', 'ctx'), may hold values from -6 to 6
- patch_order: int32 [8, 4, 128], P('dp', 'ctx'), may hold values from 0 to 127, each once within a row
- block_mask: int32 [8, 16, 8], P('dp', 'ctx'), may hold values 0 or 1
- out_weight: bfloat16 [1024, 1024], P('dp'), may hold values from -0.1875 to 0.1875
- cotangent: bfloat16 [8, 512, 1024], P('dp', 'ctx'), may hold values from -6 to 6
Outputs:
- mixed: bfloat16 [8, 512, 1024], P('dp', 'ctx')
- grad_queries: bfloat16 [8, 512, 1024], P('dp', 'ctx')
- grad_keys: bfloat16 [8, 512, 256], P('dp', 'ctx')
- grad_values: bfloat16 [8, 512, 256], P('dp', 'ctx')
- grad_weight: float32 [1024, 1024], P('dp', 'ctx')
The draws below stay inside these ranges and needn't reach their ends.
Inputs may be any that keep to these rules, and one draw needn't show every extreme that they name: `patch_order`: each row of 128 entries is a permutation.
All inputs are finite; a program needn't handle non-finite values. No bound on the sum of `block_mask` on one device may be relied on, other than what follows from the above.
Results may differ from the reference program's by a relative error of at most 0.015.
Values may be sent and summed in bfloat16 or wider, within the bound.
No kernel may reach another device: no remote copies, remote signals or barrier semaphores. Data moves between devices by JAX's collectives and lax.ppermute only.
A program may use at most 64 MiB of HBM per device.

```python
import math
import jax
import jax.numpy as jnp
from jax import lax

D = 1024
QUERY_HEADS = 8
KEY_VALUE_HEADS = 2
HEAD_WIDTH = 128
BLK = 32
TILE_TOKENS = 128
SEQS = 8
LEN = 512
HW = 1024
KVW = 256
N_CTX = 4


def draw_queries(key, part):
    drawn = jnp.clip(jax.random.normal(jax.random.fold_in(key, 1), (SEQS, LEN, HW), jnp.float32), -4.0, 4.0)
    return drawn.astype(jnp.bfloat16)


def draw_keys_in(key, part):
    drawn = jnp.clip(jax.random.normal(jax.random.fold_in(key, 13), (SEQS, LEN, KVW), jnp.float32), -4.0, 4.0)
    return drawn.astype(jnp.bfloat16)


def touch_ends(values, key, least, high):
    longest = values.shape.index(max(values.shape))
    spots = []
    for shift in (0, 1):
        where = [jax.random.randint(jax.random.fold_in(key, axis), (), 0, length) for axis, length in enumerate(values.shape)]
        where[longest] = (where[longest] + shift) % values.shape[longest]
        spots.append(tuple(where))
    return values.at[spots[0]].set(least).at[spots[1]].set(high)


def steps_of(key, shape, split, smallest, top_value):
    def one(axis_at, blocks):
        draws = jax.random.uniform(jax.random.fold_in(jax.random.fold_in(key, 6), axis_at), (blocks,), jnp.float32, smallest / len(split), top_value / len(split))
        return jnp.repeat(jnp.exp(draws), shape[axis_at] // blocks).reshape((-1,) + (1,) * (len(shape) - axis_at - 1))

    factor_of = one(*split[0])
    for cut in split[1:]:
        factor_of = factor_of * one(*cut)
    return factor_of


def noise(rng, extent, deviation, most, split=(), kind=jnp.bfloat16):
    drawn = jax.random.normal(rng, extent, jnp.float32) * deviation
    if len(split) > 0:
        drawn = steps_of(rng, extent, split, -0.22, 0.18) * drawn
    return jnp.clip(drawn, min=-most, max=most).astype(kind)


def setup_inputs(seed: int = 0) -> dict:
    splits = jax.random.split(jax.random.key(seed), 8)
    queries = draw_queries(jax.random.fold_in(splits[7], 71), 0)
    keys_in = draw_keys_in(jax.random.fold_in(splits[7], 71), 0)
    values_in = noise(splits[2], (SEQS, LEN, KVW), 1.0, 6.0, ((0, 8), (1, 4)))
    patch_order = jax.vmap(lambda own: jax.random.permutation(own, TILE_TOKENS))(jax.random.split(splits[3], SEQS * N_CTX)).reshape((SEQS, N_CTX, TILE_TOKENS)).astype(jnp.int32)
    block_mask = touch_ends((jax.random.randint(splits[4], (SEQS, LEN // BLK, 2 * TILE_TOKENS // BLK), 0, 4) < 3).astype(jnp.int32), jax.random.fold_in(splits[4], 1), 0, 1)
    out_weight = noise(splits[5], (HW, D), HW ** -0.5, 0.1875, ((0, 8),))
    cotangent = noise(splits[6], (SEQS, LEN, D), 1.0, 6.0, ((0, 8), (1, 4)))
    return dict(queries=queries, keys_in=keys_in, values_in=values_in, patch_order=patch_order, block_mask=block_mask, out_weight=out_weight, cotangent=cotangent)


def settle_band(band_parts):
    wide = band_parts.astype(jnp.float32)
    own_part = wide[:, TILE_TOKENS:2 * TILE_TOKENS]
    from_right = jnp.roll(wide[:, :TILE_TOKENS], -1, 0)
    from_left = jnp.roll(wide[:, 2 * TILE_TOKENS:], 1, 0)
    return (own_part + from_right + from_left).astype(jnp.bfloat16).reshape(LEN, KVW)

def reference(queries, keys_in, values_in, patch_order, block_mask, out_weight, cotangent):
    scale = 1.0 / math.sqrt(HEAD_WIDTH)
    query_group = QUERY_HEADS // KEY_VALUE_HEADS

    def one_sequence(carry, inputs):
        query_buffer, key_buffer, value_buffer, order_rows, mask_rows, dy_store = inputs
        offsets = (jnp.arange(N_CTX, dtype=jnp.int32) * TILE_TOKENS)[:, None]
        row_position = (order_rows.astype(jnp.int32) + offsets).reshape(-1).astype(jnp.int32)
        query_sequence = query_buffer[row_position].reshape(N_CTX, TILE_TOKENS, KEY_VALUE_HEADS, query_group, HEAD_WIDTH)
        key_sequence = key_buffer[row_position].reshape(N_CTX, TILE_TOKENS, KEY_VALUE_HEADS, HEAD_WIDTH)
        value_sequence = value_buffer[row_position].reshape(N_CTX, TILE_TOKENS, KEY_VALUE_HEADS, HEAD_WIDTH)
        key_band = jnp.concatenate([jnp.roll(key_sequence, 1, 0), key_sequence, jnp.roll(key_sequence, -1, 0)], 1)
        value_band = jnp.concatenate([jnp.roll(value_sequence, 1, 0), value_sequence, jnp.roll(value_sequence, -1, 0)], 1)
        mask_tiles = mask_rows.reshape(N_CTX, TILE_TOKENS // BLK, 2 * TILE_TOKENS // BLK)
        expanded = jnp.repeat(jnp.repeat(mask_tiles, BLK, 1), BLK, 2) > 0
        allowed = jnp.concatenate([expanded[:, :, :TILE_TOKENS], jnp.ones((N_CTX, TILE_TOKENS, TILE_TOKENS), bool), expanded[:, :, TILE_TOKENS:]], 2)
        allowed = allowed[:, None, None]
        scores = jnp.einsum('ctkgd,cskd->ckgts', query_sequence.astype(jnp.float32), key_band.astype(jnp.float32)) * scale
        scores = jnp.where(allowed, scores, -1e+30)
        highest = lax.optimization_barrier(jnp.max(scores, axis=-1, keepdims=True))
        weights = jnp.where(allowed, jnp.exp(scores - highest), 0.0)
        probs = weights / lax.optimization_barrier(jnp.sum(weights, axis=-1, keepdims=True))
        probs_b = probs.astype(jnp.bfloat16)
        attended_f = jnp.einsum('ckgts,cskd->ctkgd', probs_b.astype(jnp.float32), value_band.astype(jnp.float32))
        attended = attended_f.astype(jnp.bfloat16).reshape(LEN, HW)
        mixed_seq = jnp.dot(attended, out_weight, preferred_element_type=jnp.float32).astype(jnp.bfloat16)
        mixed_out = jnp.zeros((LEN, D), jnp.bfloat16).at[row_position].set(mixed_seq)
        dy_seq = dy_store[row_position]
        attention_gradient = jnp.dot(dy_seq, out_weight.T, preferred_element_type=jnp.float32).astype(jnp.bfloat16)
        grad_part = jnp.dot(attended.T, dy_seq, preferred_element_type=jnp.float32)
        attention_gradient5 = attention_gradient.reshape(N_CTX, TILE_TOKENS, KEY_VALUE_HEADS, query_group, HEAD_WIDTH)
        d_probs = jnp.einsum('ctkgd,cskd->ckgts', attention_gradient5.astype(jnp.float32), value_band.astype(jnp.float32))
        delta = lax.optimization_barrier(jnp.sum(attention_gradient5.astype(jnp.float32) * attended_f, axis=-1))
        delta = jnp.transpose(delta, (0, 2, 3, 1))[..., None]
        d_scores_b = (probs * (d_probs - delta)).astype(jnp.bfloat16)
        grad_q_seq = (jnp.einsum('ckgts,cskd->ctkgd', d_scores_b.astype(jnp.float32), key_band.astype(jnp.float32)) * scale).astype(jnp.bfloat16).reshape(LEN, HW)
        part_k = (jnp.einsum('ckgts,ctkgd->cskd', d_scores_b.astype(jnp.float32), query_sequence.astype(jnp.float32)) * scale).astype(jnp.bfloat16)
        part_v = jnp.einsum('ckgts,ctkgd->cskd', probs_b.astype(jnp.float32), attention_gradient5.astype(jnp.float32)).astype(jnp.bfloat16)
        grad_q_out = jnp.zeros((LEN, HW), jnp.bfloat16).at[row_position].set(grad_q_seq)
        grad_k_out = jnp.zeros((LEN, KVW), jnp.bfloat16).at[row_position].set(settle_band(part_k))
        grad_v_out = jnp.zeros((LEN, KVW), jnp.bfloat16).at[row_position].set(settle_band(part_v))
        return (carry + grad_part, (mixed_out, grad_q_out, grad_k_out, grad_v_out))
    start_total = jnp.zeros((HW, D), jnp.float32)
    total, outputs = lax.scan(one_sequence, start_total, (queries, keys_in, values_in, patch_order, block_mask, cotangent))
    grad_weight = total * (1.0 / math.sqrt(SEQS * LEN))
    return (outputs[0], outputs[1], outputs[2], outputs[3], grad_weight)
```

```python
import functools
import math

import jax
import jax.numpy as jnp
from jax import lax
from jax.experimental import pallas as pl
from jax.experimental.pallas import tpu as pltpu
from jax.sharding import PartitionSpec as P

QUERY_HEADS = 8
KEY_VALUE_HEADS = 2
HEAD_WIDTH = 128
BLK = 32
HALO_ROWS = 8


F32 = jnp.float32
BF16 = jnp.bfloat16
NN = (((1,), (0,)), ((), ()))
NT = (((1,), (1,)), ((), ()))
TN = (((0,), (0,)), ((), ()))


def dot(a, b, dims):
    return lax.dot_general(a, b, dims, preferred_element_type=F32)


def vmem():
    return pl.BlockSpec(memory_space=pltpu.VMEM)


def smem():
    return pl.BlockSpec(memory_space=pltpu.SMEM)


def call(body, name, outs, specs, args, scratch=(), flops=1 << 20, room=16 << 20):
    moved = sum(a.size * a.dtype.itemsize for a in (*args, *outs))
    return pl.pallas_call(
        body,
        name=name,
        out_shape=outs,
        in_specs=specs,
        out_specs=[vmem() for _ in outs],
        scratch_shapes=list(scratch),
        cost_estimate=pl.CostEstimate(flops=flops, bytes_accessed=moved, transcendentals=0),
        compiler_params=pltpu.CompilerParams(vmem_limit_bytes=room),
    )(*args)


def shape(dims, dtype=BF16):
    return jax.ShapeDtypeStruct(dims, dtype)


def pack_body(k_ref, v_ref, order_ref, out_ref):
    tokens, width = k_ref.shape
    out_ref[:tokens, :width] = k_ref[...]
    out_ref[:tokens, width:] = v_ref[...]
    row = lax.broadcasted_iota(jnp.int32, (tokens, tokens), 0)
    holds = (row == order_ref[...]).astype(F32).astype(BF16)
    block = lax.broadcasted_iota(jnp.int32, (HALO_ROWS, tokens), 1) // BLK
    out_ref[tokens:, :] = jnp.zeros((HALO_ROWS, 2 * width), BF16)
    out_ref[tokens:, :tokens] = dot(block.astype(F32).astype(BF16), holds, NT).astype(BF16)


def seen(mask_ref, first, key_block, query_block):
    sub = lax.broadcasted_iota(jnp.int32, key_block.shape, 0)
    blocks = mask_ref.shape[1] // 2
    table = jnp.zeros(key_block.shape, F32)
    for b in range(mask_ref.shape[0]):
        for kb in range(blocks):
            here = (sub == b) & (key_block == kb)
            table = jnp.where(here, mask_ref[b, first + kb].astype(F32), table)
    one_hot = (sub == query_block).astype(F32)
    return dot(table.astype(BF16), one_hot.astype(BF16), TN)


def forward_body(scale, q_ref, prev_ref, own_ref, next_ref, mask_ref, prob_ref, attf_ref, att_ref):
    tokens = q_ref.shape[0]
    width = own_ref.shape[1] // 2
    group = QUERY_HEADS // KEY_VALUE_HEADS
    blocks = mask_ref.shape[1] // 2
    ids = [r[tokens:, :tokens].astype(F32).astype(jnp.int32) for r in (prev_ref, own_ref, next_ref)]
    see_prev = seen(mask_ref, 0, ids[0], ids[1]) > 0.5
    see_next = seen(mask_ref, blocks, ids[2], ids[1]) > 0.5
    for g in range(KEY_VALUE_HEADS):
        cols = slice(g * HEAD_WIDTH, (g + 1) * HEAD_WIDTH)
        vcols = slice(width + g * HEAD_WIDTH, width + (g + 1) * HEAD_WIDTH)
        keys = jnp.concatenate([r[:tokens, cols] for r in (prev_ref, own_ref, next_ref)], 0)
        values = jnp.concatenate([r[:tokens, vcols] for r in (prev_ref, own_ref, next_ref)], 0)
        values_t = values.T
        for j in range(group):
            h = g * group + j
            at = slice(h * HEAD_WIDTH, (h + 1) * HEAD_WIDTH)
            scores = dot(keys, q_ref[:, at], NT) * scale
            low = jnp.where(see_prev, scores[:tokens], -1e30)
            mid = scores[tokens : 2 * tokens]
            high = jnp.where(see_next, scores[2 * tokens :], -1e30)
            top = jnp.maximum(jnp.maximum(low, mid), high).max(axis=0, keepdims=True)
            low, mid, high = jnp.exp(low - top), jnp.exp(mid - top), jnp.exp(high - top)
            inverse = 1.0 / (low + mid + high).sum(axis=0, keepdims=True)
            prob = jnp.concatenate([(low * inverse), (mid * inverse), (high * inverse)], 0).astype(BF16)
            prob_ref[:, at] = prob
            att = dot(values_t, prob, NN)
            attf_ref[at, :] = att
            att_ref[at, :] = att.astype(BF16)


def split_body(att_ref, keep_ref, send_ref):
    mine = lax.rem(lax.axis_index("dp"), 2)
    for z in range(QUERY_HEADS // 2):
        to = slice(z * HEAD_WIDTH, (z + 1) * HEAD_WIDTH)
        keep = pl.multiple_of((2 * z + mine) * HEAD_WIDTH, HEAD_WIDTH)
        send = pl.multiple_of((2 * z + 1 - mine) * HEAD_WIDTH, HEAD_WIDTH)
        keep_ref[to, :] = att_ref[pl.ds(keep, HEAD_WIDTH), :]
        send_ref[to, :] = att_ref[pl.ds(send, HEAD_WIDTH), :]


def weight_part_body(parts, keep_ref, other_ref, dy_ref, dy_other_ref, *outs):
    me = lax.axis_index("ctx")
    cols = dy_ref.shape[1] // parts
    left = jnp.concatenate([keep_ref[...], other_ref[...]], 1)
    for m, out in enumerate(outs):
        at = pl.ds(pl.multiple_of((me ^ m) * cols, cols), cols)
        right = jnp.concatenate([dy_ref[:, at], dy_other_ref[:, at]], 0)
        out[...] = dot(left, right, NN).astype(out.dtype)


def weight_plane_body(count, *refs):
    ins, outs = refs[:count], refs[count:]
    me = lax.axis_index("dp") // 2
    rows = outs[0].shape[0]
    for m, out in enumerate(outs):
        at = pl.ds(pl.multiple_of((me ^ m) * rows, rows), rows)
        total = ins[0][at, :].astype(F32)
        for r in ins[1:]:
            total = total + r[at, :].astype(F32)
        out[...] = total.astype(out.dtype)


def weight_sum_body(factor, *refs):
    total = refs[0][...].astype(F32)
    for r in refs[1:-1]:
        total = total + r[...].astype(F32)
    refs[-1][...] = total * factor


def load_weight(pieces, w_scr, sem, block_of):
    copies = [
        pltpu.make_async_copy(p, w_scr.at[block_of(j)], sem.at[j]) for j, p in enumerate(pieces)
    ]
    for c in copies:
        c.start()
    for c in copies:
        c.wait()


def backward_body(
    scale, pieces, block_of, q_ref, prev_ref, own_ref, next_ref, dy_ref, prob_ref, attf_ref, *rest
):
    w_refs, (low_ref, mid_ref, high_ref, ds_ref, w_scr, dat_scr, sem) = rest[:pieces], rest[pieces:]
    load_weight(w_refs, w_scr, sem, block_of())
    tokens = q_ref.shape[0]
    width = own_ref.shape[1] // 2
    group = QUERY_HEADS // KEY_VALUE_HEADS
    weight = w_scr[...].reshape(QUERY_HEADS * HEAD_WIDTH, dy_ref.shape[1])
    dat_scr[...] = dot(weight, dy_ref[...], NT).astype(BF16)
    for g in range(KEY_VALUE_HEADS):
        cols = slice(g * HEAD_WIDTH, (g + 1) * HEAD_WIDTH)
        vcols = slice(width + g * HEAD_WIDTH, width + (g + 1) * HEAD_WIDTH)
        values = jnp.concatenate([r[:tokens, vcols] for r in (prev_ref, own_ref, next_ref)], 0)
        for j in range(group):
            h = g * group + j
            at = slice(h * HEAD_WIDTH, (h + 1) * HEAD_WIDTH)
            dat = dat_scr[at, :]
            delta = (dat.astype(F32) * attf_ref[at, :]).sum(axis=0, keepdims=True)
            dprob = dot(values, dat, NN)
            ds_ref[:, at] = (prob_ref[:, at].astype(F32) * (dprob - delta)).astype(BF16)
        heads = slice(g * group * HEAD_WIDTH, (g + 1) * group * HEAD_WIDTH)
        q_rows = jnp.concatenate(
            [q_ref[:, (g * group + j) * HEAD_WIDTH : (g * group + j + 1) * HEAD_WIDTH] for j in range(group)], 0
        )
        part_k = (dot(ds_ref[:, heads], q_rows, NN) * scale).astype(BF16)
        d_rows = jnp.concatenate(
            [dat_scr[(g * group + j) * HEAD_WIDTH : (g * group + j + 1) * HEAD_WIDTH, :].T for j in range(group)], 0
        )
        part_v = dot(prob_ref[:, heads], d_rows, NN).astype(BF16)
        for t, out in enumerate((low_ref, mid_ref, high_ref)):
            out[:, cols] = part_k[t * tokens : (t + 1) * tokens]
            out[:, vcols] = part_v[t * tokens : (t + 1) * tokens]


def output_body(
    scale, pieces, block_of, prev_ref, own_ref, next_ref, ds_ref, att_ref, *rest
):
    w_refs, (mixed_ref, gq_ref, w_scr, sem) = rest[:pieces], rest[pieces:]
    load_weight(w_refs, w_scr, sem, block_of())
    tokens = mixed_ref.shape[0]
    group = QUERY_HEADS // KEY_VALUE_HEADS
    for g in range(KEY_VALUE_HEADS):
        cols = slice(g * HEAD_WIDTH, (g + 1) * HEAD_WIDTH)
        keys = jnp.concatenate([r[:tokens, cols] for r in (prev_ref, own_ref, next_ref)], 0)
        heads = slice(g * group * HEAD_WIDTH, (g + 1) * group * HEAD_WIDTH)
        dq = dot(keys.T, ds_ref[:, heads], NN) * scale
        for j in range(group):
            h = g * group + j
            at = slice(h * HEAD_WIDTH, (h + 1) * HEAD_WIDTH)
            gq_ref[:, at] = dq[:, j * tokens : (j + 1) * tokens].T.astype(BF16)
    weight = w_scr[...].reshape(QUERY_HEADS * HEAD_WIDTH, mixed_ref.shape[1])
    att = jnp.concatenate(
        [att_ref[h * HEAD_WIDTH : (h + 1) * HEAD_WIDTH, :].T for h in range(QUERY_HEADS)], 1
    )
    mixed_ref[...] = dot(att, weight, NN).astype(BF16)


def key_value_body(own_ref, low_ref, high_ref, gk_ref, gv_ref):
    width = gk_ref.shape[1]
    total = own_ref[...].astype(F32) + low_ref[...].astype(F32) + high_ref[...].astype(F32)
    gk_ref[...] = total[:, :width].astype(BF16)
    gv_ref[...] = total[:, width:].astype(BF16)


def power_of_two(n):
    return n & (n - 1) == 0


def flip(value, axis, mask):
    return lax.ppermute(value, axis, [(i, i ^ mask) for i in range(lax.axis_size(axis))])


def turn(value, axis, step):
    count = lax.axis_size(axis)
    return lax.ppermute(value, axis, [(i, (i + step) % count) for i in range(count)])


def shards(queries, keys_in, values_in, patch_order, block_mask, out_weight, cotangent):
    scale = 1.0 / math.sqrt(HEAD_WIDTH)
    n_dp, n_ctx = lax.axis_size("dp"), lax.axis_size("ctx")
    q, k, v, dy = queries[0], keys_in[0], values_in[0], cotangent[0]
    tokens, query_width = q.shape
    kv_width = k.shape[1]
    model = dy.shape[1]
    band = 3 * tokens
    by_head = n_dp == QUERY_HEADS
    column_width = model // n_ctx
    staged = by_head and power_of_two(n_ctx) and column_width % 128 == 0
    macs = tokens * query_width

    own = call(
        pack_body, "pack", [shape((tokens + HALO_ROWS, 2 * kv_width))], [vmem()] * 3, (k, v, patch_order[0])
    )[0]
    prev_kv = turn(own, "ctx", 1)
    next_kv = turn(own, "ctx", -1)

    if by_head:
        pieces = []
        for j in range(0, n_dp, 2):
            piece = flip(out_weight, "dp", j) if j else out_weight
            pieces += [piece, flip(piece, "dp", 1)]

        def block_of():
            me = lax.axis_index("dp")
            return lambda j: me ^ j
    else:
        weight_all = lax.all_gather(out_weight, "dp", axis=0, tiled=True)
        pieces = [weight_all.reshape(QUERY_HEADS, HEAD_WIDTH, model)[h] for h in range(QUERY_HEADS)]

        def block_of():
            return lambda j: j

    prob, attf, att = call(
        functools.partial(forward_body, scale),
        "forward",
        [shape((band, query_width)), shape((query_width, tokens), F32), shape((query_width, tokens))],
        [vmem()] * 4 + [smem()],
        (q, prev_kv, own, next_kv, block_mask[0]),
        flops=4 * macs * band,
    )

    total_tokens = n_dp * tokens * n_ctx
    norm_factor = 1.0 / math.sqrt(total_tokens)
    if staged:
        dy_other = flip(dy, "dp", 1)
        half = query_width // 2
        keep, send = call(split_body, "split", [shape((half, tokens))] * 2, [vmem()], (att,))
        other = flip(send, "dp", 1)
        parts = call(
            functools.partial(weight_part_body, n_ctx),
            "weight_part",
            [shape((half, column_width))] * n_ctx,
            [vmem()] * 4,
            (keep, other, dy, dy_other),
            flops=2 * half * 2 * tokens * model,
        )
        arrived = [parts[0]] + [flip(parts[m], "ctx", m) for m in range(1, n_ctx)]
        n_z = n_dp // 2
        blocks = call(
            functools.partial(weight_plane_body, n_ctx),
            "weight_plane",
            [shape((half // n_z, column_width))] * n_z,
            [vmem()] * n_ctx,
            arrived,
        )
        landed = [blocks[0]] + [flip(blocks[m], "dp", 2 * m) for m in range(1, n_z)]
        grad_weight = call(
            functools.partial(weight_sum_body, norm_factor),
            "weight_sum",
            [shape((half // n_z, column_width), F32)],
            [vmem()] * n_z,
            landed,
        )[0]
    else:
        part = dot(att, dy, NN).astype(BF16)
        columns = lax.psum_scatter(part, "ctx", scatter_dimension=1, tiled=True).astype(F32)
        grad_weight = lax.psum_scatter(columns, "dp", scatter_dimension=0, tiled=True) * norm_factor

    anywhere = [pl.BlockSpec(memory_space=pl.ANY)] * QUERY_HEADS
    w_scratch = [
        pltpu.VMEM((QUERY_HEADS, HEAD_WIDTH, model), BF16),
    ]
    sems = [pltpu.SemaphoreType.DMA((QUERY_HEADS,))]
    low, mid, high, ds = call(
        functools.partial(backward_body, scale, QUERY_HEADS, block_of),
        "backward",
        [shape((tokens, 2 * kv_width))] * 3 + [shape((band, query_width))],
        [vmem()] * 7 + anywhere,
        (q, prev_kv, own, next_kv, dy, prob, attf, *pieces),
        scratch=w_scratch + [pltpu.VMEM((query_width, tokens), BF16)] + sems,
        flops=2 * macs * model + 6 * macs * band,
    )
    from_next = turn(low, "ctx", -1)
    from_prev = turn(high, "ctx", 1)
    mixed, grad_q = call(
        functools.partial(output_body, scale, QUERY_HEADS, block_of),
        "output",
        [shape((tokens, model)), shape((tokens, query_width))],
        [vmem()] * 5 + anywhere,
        (prev_kv, own, next_kv, ds, att, *pieces),
        scratch=w_scratch + sems,
        flops=2 * macs * model + 2 * macs * band,
    )
    grad_k, grad_v = call(
        key_value_body, "key_value", [shape((tokens, kv_width))] * 2, [vmem()] * 3, (mid, from_next, from_prev)
    )
    return (mixed[None], grad_q[None], grad_k[None], grad_v[None], grad_weight)


def solution(mesh):
    row = P("dp", "ctx", None)
    in_specs = (row, row, row, row, row, P("dp", None), row)
    out_specs = (row, row, row, row, P("dp", "ctx"))
    return jax.shard_map(shards, mesh=mesh, in_specs=in_specs, out_specs=out_specs, check_vma=False)
```

```python
import functools
import math

import jax
import jax.numpy as jnp
from jax import lax
from jax.experimental import pallas as pl
from jax.experimental.pallas import tpu as pltpu
from jax.sharding import PartitionSpec as P

QUERY_HEADS = 8
KEY_VALUE_HEADS = 2
HEAD_WIDTH = 128
BLK = 32
HALO_ROWS = 8


F32 = jnp.float32
BF16 = jnp.bfloat16
NN = (((1,), (0,)), ((), ()))
NT = (((1,), (1,)), ((), ()))
TN = (((0,), (0,)), ((), ()))


def dot(a, b, dims):
    return lax.dot_general(a, b, dims, preferred_element_type=F32)


def vmem():
    return pl.BlockSpec(memory_space=pltpu.VMEM)


def smem():
    return pl.BlockSpec(memory_space=pltpu.SMEM)


def hbm():
    return pl.BlockSpec(memory_space=pltpu.HBM)


def in_hbm(*arrays):
    return tuple(pltpu.with_memory_space_constraint(a, pltpu.HBM) for a in arrays)


def call(body, outs, specs, args, scratch=(), flops=1 << 20, room=16 << 20):
    moved = sum(a.size * a.dtype.itemsize for a in (*args, *outs))
    return pl.pallas_call(
        body,
        out_shape=outs,
        in_specs=specs,
        out_specs=[vmem() for _ in outs],
        scratch_shapes=list(scratch),
        cost_estimate=pl.CostEstimate(flops=flops, bytes_accessed=moved, transcendentals=0),
        compiler_params=pltpu.CompilerParams(vmem_limit_bytes=room),
    )(*args)


def shape(dims, dtype=BF16):
    return jax.ShapeDtypeStruct(dims, dtype)


def pack_body(k_ref, v_ref, order_ref, out_ref, order_scr, sem):
    tokens, width = k_ref.shape
    copies = [
        pltpu.make_async_copy(order_ref, order_scr, sem.at[0]),
        pltpu.make_async_copy(k_ref, out_ref.at[:tokens, :width], sem.at[1]),
        pltpu.make_async_copy(v_ref, out_ref.at[:tokens, width:], sem.at[2]),
    ]
    for c in copies:
        c.start()
    copies[0].wait()
    row = lax.broadcasted_iota(jnp.int32, (tokens, tokens), 0)
    holds = (row == order_scr[...]).astype(F32).astype(BF16)
    block = lax.broadcasted_iota(jnp.int32, (HALO_ROWS, tokens), 1) // BLK
    out_ref[tokens:, :] = jnp.zeros((HALO_ROWS, 2 * width), BF16)
    out_ref[tokens:, :tokens] = dot(block.astype(F32).astype(BF16), holds, NT).astype(BF16)
    copies[1].wait()
    copies[2].wait()


def fetch_body(a_ref, b_ref, a_out, b_out, sem):
    copies = [
        pltpu.make_async_copy(a_ref, a_out, sem.at[0]),
        pltpu.make_async_copy(b_ref, b_out, sem.at[1]),
    ]
    for c in copies:
        c.start()
    for c in copies:
        c.wait()


def seen(mask_ref, first, key_block, query_block):
    sub = lax.broadcasted_iota(jnp.int32, key_block.shape, 0)
    blocks = mask_ref.shape[1] // 2
    table = jnp.zeros(key_block.shape, F32)
    for b in range(mask_ref.shape[0]):
        for kb in range(blocks):
            here = (sub == b) & (key_block == kb)
            table = jnp.where(here, mask_ref[b, first + kb].astype(F32), table)
    one_hot = (sub == query_block).astype(F32)
    return dot(table.astype(BF16), one_hot.astype(BF16), TN)


def forward_body(scale, q_ref, prev_ref, own_ref, next_ref, mask_ref, prob_ref, attf_ref, att_ref):
    tokens = q_ref.shape[0]
    width = own_ref.shape[1] // 2
    group = QUERY_HEADS // KEY_VALUE_HEADS
    blocks = mask_ref.shape[1] // 2
    ids = [r[tokens:, :tokens].astype(F32).astype(jnp.int32) for r in (prev_ref, own_ref, next_ref)]
    see_prev = seen(mask_ref, 0, ids[0], ids[1]) > 0.5
    see_next = seen(mask_ref, blocks, ids[2], ids[1]) > 0.5
    for g in range(KEY_VALUE_HEADS):
        cols = slice(g * HEAD_WIDTH, (g + 1) * HEAD_WIDTH)
        vcols = slice(width + g * HEAD_WIDTH, width + (g + 1) * HEAD_WIDTH)
        keys = jnp.concatenate([r[:tokens, cols] for r in (prev_ref, own_ref, next_ref)], 0)
        values = jnp.concatenate([r[:tokens, vcols] for r in (prev_ref, own_ref, next_ref)], 0)
        values_t = values.T
        for j in range(group):
            h = g * group + j
            at = slice(h * HEAD_WIDTH, (h + 1) * HEAD_WIDTH)
            scores = dot(keys, q_ref[:, at], NT) * scale
            low = jnp.where(see_prev, scores[:tokens], -1e30)
            mid = scores[tokens : 2 * tokens]
            high = jnp.where(see_next, scores[2 * tokens :], -1e30)
            top = jnp.maximum(jnp.maximum(low, mid), high).max(axis=0, keepdims=True)
            low, mid, high = jnp.exp(low - top), jnp.exp(mid - top), jnp.exp(high - top)
            inverse = 1.0 / (low + mid + high).sum(axis=0, keepdims=True)
            prob = jnp.concatenate([(low * inverse), (mid * inverse), (high * inverse)], 0).astype(BF16)
            prob_ref[:, at] = prob
            att = dot(values_t, prob, NN)
            attf_ref[at, :] = att
            att_ref[at, :] = att.astype(BF16)


def split_body(att_ref, keep_ref, send_ref):
    mine = lax.rem(lax.axis_index("dp"), 2)
    for z in range(QUERY_HEADS // 2):
        to = slice(z * HEAD_WIDTH, (z + 1) * HEAD_WIDTH)
        keep = pl.multiple_of((2 * z + mine) * HEAD_WIDTH, HEAD_WIDTH)
        send = pl.multiple_of((2 * z + 1 - mine) * HEAD_WIDTH, HEAD_WIDTH)
        keep_ref[to, :] = att_ref[pl.ds(keep, HEAD_WIDTH), :]
        send_ref[to, :] = att_ref[pl.ds(send, HEAD_WIDTH), :]


def weight_part_body(parts, keep_ref, other_ref, dy_ref, dy_other_ref, *outs):
    me = lax.axis_index("ctx")
    cols = dy_ref.shape[1] // parts
    left = jnp.concatenate([keep_ref[...], other_ref[...]], 1)
    for m, out in enumerate(outs):
        at = pl.ds(pl.multiple_of((me ^ m) * cols, cols), cols)
        right = jnp.concatenate([dy_ref[:, at], dy_other_ref[:, at]], 0)
        out[...] = dot(left, right, NN).astype(out.dtype)


def weight_plane_body(count, *refs):
    ins, outs = refs[:count], refs[count:]
    me = lax.axis_index("dp") // 2
    rows = outs[0].shape[0]
    for m, out in enumerate(outs):
        at = pl.ds(pl.multiple_of((me ^ m) * rows, rows), rows)
        total = ins[0][at, :].astype(F32)
        for r in ins[1:]:
            total = total + r[at, :].astype(F32)
        out[...] = total.astype(out.dtype)


def weight_sum_body(factor, *refs):
    total = refs[0][...].astype(F32)
    for r in refs[1:-1]:
        total = total + r[...].astype(F32)
    refs[-1][...] = total * factor


def load_weight(pieces, w_scr, sem, block_of):
    copies = [
        pltpu.make_async_copy(p, w_scr.at[block_of(j)], sem.at[j]) for j, p in enumerate(pieces)
    ]
    for c in copies:
        c.start()
    for c in copies:
        c.wait()


def backward_body(
    scale, pieces, block_of, q_ref, prev_ref, own_ref, next_ref, dy_ref, prob_ref, attf_ref, *rest
):
    w_refs, (low_ref, mid_ref, high_ref, ds_ref, w_scr, dat_scr, sem) = rest[:pieces], rest[pieces:]
    load_weight(w_refs, w_scr, sem, block_of())
    tokens = q_ref.shape[0]
    width = own_ref.shape[1] // 2
    group = QUERY_HEADS // KEY_VALUE_HEADS
    weight = w_scr[...].reshape(QUERY_HEADS * HEAD_WIDTH, dy_ref.shape[1])
    dat_scr[...] = dot(weight, dy_ref[...], NT).astype(BF16)
    for g in range(KEY_VALUE_HEADS):
        cols = slice(g * HEAD_WIDTH, (g + 1) * HEAD_WIDTH)
        vcols = slice(width + g * HEAD_WIDTH, width + (g + 1) * HEAD_WIDTH)
        values = jnp.concatenate([r[:tokens, vcols] for r in (prev_ref, own_ref, next_ref)], 0)
        for j in range(group):
            h = g * group + j
            at = slice(h * HEAD_WIDTH, (h + 1) * HEAD_WIDTH)
            dat = dat_scr[at, :]
            delta = (dat.astype(F32) * attf_ref[at, :]).sum(axis=0, keepdims=True)
            dprob = dot(values, dat, NN)
            ds_ref[:, at] = (prob_ref[:, at].astype(F32) * (dprob - delta)).astype(BF16)
        heads = slice(g * group * HEAD_WIDTH, (g + 1) * group * HEAD_WIDTH)
        q_rows = jnp.concatenate(
            [q_ref[:, (g * group + j) * HEAD_WIDTH : (g * group + j + 1) * HEAD_WIDTH] for j in range(group)], 0
        )
        part_k = (dot(ds_ref[:, heads], q_rows, NN) * scale).astype(BF16)
        d_rows = jnp.concatenate(
            [dat_scr[(g * group + j) * HEAD_WIDTH : (g * group + j + 1) * HEAD_WIDTH, :].T for j in range(group)], 0
        )
        part_v = dot(prob_ref[:, heads], d_rows, NN).astype(BF16)
        for t, out in enumerate((low_ref, mid_ref, high_ref)):
            out[:, cols] = part_k[t * tokens : (t + 1) * tokens]
            out[:, vcols] = part_v[t * tokens : (t + 1) * tokens]


def output_body(
    scale, pieces, block_of, prev_ref, own_ref, next_ref, ds_ref, att_ref, *rest
):
    w_refs, (mixed_ref, gq_ref, w_scr, sem) = rest[:pieces], rest[pieces:]
    load_weight(w_refs, w_scr, sem, block_of())
    tokens = mixed_ref.shape[0]
    group = QUERY_HEADS // KEY_VALUE_HEADS
    for g in range(KEY_VALUE_HEADS):
        cols = slice(g * HEAD_WIDTH, (g + 1) * HEAD_WIDTH)
        keys = jnp.concatenate([r[:tokens, cols] for r in (prev_ref, own_ref, next_ref)], 0)
        heads = slice(g * group * HEAD_WIDTH, (g + 1) * group * HEAD_WIDTH)
        dq = dot(keys.T, ds_ref[:, heads], NN) * scale
        for j in range(group):
            h = g * group + j
            at = slice(h * HEAD_WIDTH, (h + 1) * HEAD_WIDTH)
            gq_ref[:, at] = dq[:, j * tokens : (j + 1) * tokens].T.astype(BF16)
    weight = w_scr[...].reshape(QUERY_HEADS * HEAD_WIDTH, mixed_ref.shape[1])
    att = jnp.concatenate(
        [att_ref[h * HEAD_WIDTH : (h + 1) * HEAD_WIDTH, :].T for h in range(QUERY_HEADS)], 1
    )
    mixed_ref[...] = dot(att, weight, NN).astype(BF16)


def key_value_body(own_ref, low_ref, high_ref, gk_ref, gv_ref):
    width = gk_ref.shape[1]
    total = own_ref[...].astype(F32) + low_ref[...].astype(F32) + high_ref[...].astype(F32)
    gk_ref[...] = total[:, :width].astype(BF16)
    gv_ref[...] = total[:, width:].astype(BF16)


def power_of_two(n):
    return n & (n - 1) == 0


def flip(value, axis, mask):
    return lax.ppermute(value, axis, [(i, i ^ mask) for i in range(lax.axis_size(axis))])


def turn(value, axis, step):
    count = lax.axis_size(axis)
    return lax.ppermute(value, axis, [(i, (i + step) % count) for i in range(count)])


def sublayer(queries, keys_in, values_in, patch_order, block_mask, out_weight, cotangent):
    scale = 1.0 / math.sqrt(HEAD_WIDTH)
    n_dp, n_ctx = lax.axis_size("dp"), lax.axis_size("ctx")
    q, k, v, dy = queries[0], keys_in[0], values_in[0], cotangent[0]
    tokens, query_width = q.shape
    kv_width = k.shape[1]
    model = dy.shape[1]
    band = 3 * tokens
    by_head = n_dp == QUERY_HEADS
    column_width = model // n_ctx
    staged = by_head and power_of_two(n_ctx) and column_width % 128 == 0
    macs = tokens * query_width

    own = call(
        pack_body,
        [shape((tokens + HALO_ROWS, 2 * kv_width))],
        [hbm()] * 3,
        in_hbm(k, v, patch_order[0]),
        scratch=[pltpu.VMEM((1, tokens), jnp.int32), pltpu.SemaphoreType.DMA((3,))],
        room=16<<20,
    )[0]
    dy_hbm = dy
    q, dy = call(
        fetch_body, [shape(q.shape), shape(dy.shape)], [hbm()] * 2, in_hbm(q, dy),
        scratch=[pltpu.SemaphoreType.DMA((2,))],
    )
    prev_kv = turn(own, "ctx", 1)
    next_kv = turn(own, "ctx", -1)

    if by_head:
        mine = {0: out_weight}
        for j in range(n_dp // 2, 1, -2):
            mine[j] = flip(out_weight, "dp", j)
        for j in range(n_dp // 2 + 2, n_dp, 2):
            mine[j] = flip(mine[n_dp // 2], "dp", j - n_dp // 2)

        def block_of():
            me = lax.axis_index("dp")
            return lambda j: me ^ j
    else:
        weight_all = lax.all_gather(out_weight, "dp", axis=0, tiled=True)
        pieces = [weight_all.reshape(QUERY_HEADS, HEAD_WIDTH, model)[h] for h in range(QUERY_HEADS)]

        def block_of():
            return lambda j: j

    prob, attf, att = call(
        functools.partial(forward_body, scale),
        [shape((band, query_width)), shape((query_width, tokens), F32), shape((query_width, tokens))],
        [vmem()] * 4 + [smem()],
        (q, prev_kv, own, next_kv, block_mask[0]),
        flops=4 * macs * band,
    )

    total_tokens = n_dp * tokens * n_ctx
    norm_factor = 1.0 / math.sqrt(total_tokens)
    if staged:
        dy_other = flip(dy_hbm, "dp", 1)
        half = query_width // 2
        keep, send = call(split_body, [shape((half, tokens))] * 2, [vmem()], (att,))
        other = flip(send, "dp", 1)
        parts = call(
            functools.partial(weight_part_body, n_ctx),
            [shape((half, column_width))] * n_ctx,
            [vmem()] * 4,
            (keep, other, dy, dy_other),
            flops=2 * half * 2 * tokens * model,
        )
        arrived = [parts[0]]
        for m in range(1, n_ctx):
            arrived.append(flip(parts[m], "ctx", m))
        n_z = n_dp // 2
        blocks = call(
            functools.partial(weight_plane_body, n_ctx),
            [shape((half // n_z, column_width))] * n_z,
            [vmem()] * n_ctx,
            arrived,
        )
        landed = [blocks[0]]
        for m in range(1, n_z):
            landed.append(flip(blocks[m], "dp", 2 * m))
        grad_weight = call(
            functools.partial(weight_sum_body, norm_factor),
            [shape((half // n_z, column_width), F32)],
            [vmem()] * n_z,
            landed,
        )[0]
    else:
        part = dot(att, dy, NN).astype(BF16)
        columns = lax.psum_scatter(part, "ctx", scatter_dimension=1, tiled=True).astype(F32)
        grad_weight = lax.psum_scatter(columns, "dp", scatter_dimension=0, tiled=True) * norm_factor

    if by_head:
        pieces = []
        for j in range(0, n_dp, 2):
            pieces += [mine[j], flip(mine[j], "dp", 1)]

    anywhere = [pl.BlockSpec(memory_space=pl.ANY)] * QUERY_HEADS
    w_scratch = [
        pltpu.VMEM((QUERY_HEADS, HEAD_WIDTH, model), BF16),
    ]
    sems = [pltpu.SemaphoreType.DMA((QUERY_HEADS,))]
    low, mid, high, ds = call(
        functools.partial(backward_body, scale, QUERY_HEADS, block_of),
        [shape((tokens, 2 * kv_width))] * 3 + [shape((band, query_width))],
        [vmem()] * 7 + anywhere,
        (q, prev_kv, own, next_kv, dy, prob, attf, *pieces),
        scratch=w_scratch + [pltpu.VMEM((query_width, tokens), BF16)] + sems,
        flops=2 * macs * model + 6 * macs * band,
    )
    from_next = turn(low, "ctx", -1)
    from_prev = turn(high, "ctx", 1)
    mixed, grad_q = call(
        functools.partial(output_body, scale, QUERY_HEADS, block_of),
        [shape((tokens, model)), shape((tokens, query_width))],
        [vmem()] * 5 + anywhere,
        (prev_kv, own, next_kv, ds, att, *pieces),
        scratch=w_scratch + sems,
        flops=2 * macs * model + 2 * macs * band,
    )
    grad_k, grad_v = call(
        key_value_body, [shape((tokens, kv_width))] * 2, [vmem()] * 3, (mid, from_next, from_prev)
    )
    return (mixed[None], grad_q[None], grad_k[None], grad_v[None], grad_weight)


def solution(mesh):
    row = P("dp", "ctx", None)
    in_specs = (row, row, row, row, row, P("dp", None), row)
    out_specs = (row, row, row, row, P("dp", "ctx"))
    return jax.shard_map(sublayer, mesh=mesh, in_specs=in_specs, out_specs=out_specs, check_vma=False)
```

```python
import functools
import math

import jax
import jax.numpy as jnp
from jax import lax
from jax.experimental import pallas as pl
from jax.experimental.pallas import tpu as pltpu
from jax.sharding import PartitionSpec as P

QUERY_HEADS = 8
KEY_VALUE_HEADS = 2
HEAD_WIDTH = 128
BLK = 32
HALO_ROWS = 8


F32 = jnp.float32
BF16 = jnp.bfloat16
NN = (((1,), (0,)), ((), ()))
NT = (((1,), (1,)), ((), ()))
TN = (((0,), (0,)), ((), ()))


def dot(a, b, dims):
    return lax.dot_general(a, b, dims, preferred_element_type=F32)


def vmem():
    return pl.BlockSpec(memory_space=pltpu.VMEM)


def smem():
    return pl.BlockSpec(memory_space=pltpu.SMEM)


def hbm():
    return pl.BlockSpec(memory_space=pltpu.HBM)


def in_hbm(*arrays):
    return tuple(pltpu.with_memory_space_constraint(a, pltpu.HBM) for a in arrays)


def call(body, outs, specs, args, scratch=(), flops=1 << 20, room=16 << 20):
    moved = sum(a.size * a.dtype.itemsize for a in (*args, *outs))
    return pl.pallas_call(
        body,
        out_shape=outs,
        in_specs=specs,
        out_specs=[vmem() for _ in outs],
        scratch_shapes=list(scratch),
        cost_estimate=pl.CostEstimate(flops=flops, bytes_accessed=moved, transcendentals=0),
        compiler_params=pltpu.CompilerParams(vmem_limit_bytes=room),
    )(*args)


def shape(dims, dtype=BF16):
    return jax.ShapeDtypeStruct(dims, dtype)


def pack_body(k_ref, v_ref, order_ref, out_ref, order_scr, sem):
    tokens, width = k_ref.shape
    copies = [
        pltpu.make_async_copy(order_ref, order_scr, sem.at[0]),
        pltpu.make_async_copy(k_ref, out_ref.at[:tokens, :width], sem.at[1]),
        pltpu.make_async_copy(v_ref, out_ref.at[:tokens, width:], sem.at[2]),
    ]
    for c in copies:
        c.start()
    copies[0].wait()
    row = lax.broadcasted_iota(jnp.int32, (tokens, tokens), 0)
    holds = (row == order_scr[...]).astype(F32).astype(BF16)
    block = lax.broadcasted_iota(jnp.int32, (HALO_ROWS, tokens), 1) // BLK
    out_ref[tokens:, :] = jnp.zeros((HALO_ROWS, 2 * width), BF16)
    out_ref[tokens:, :tokens] = dot(block.astype(F32).astype(BF16), holds, NT).astype(BF16)
    copies[1].wait()
    copies[2].wait()


def fetch_body(a_ref, b_ref, a_out, b_out, sem):
    copies = [
        pltpu.make_async_copy(a_ref, a_out, sem.at[0]),
        pltpu.make_async_copy(b_ref, b_out, sem.at[1]),
    ]
    for c in copies:
        c.start()
    for c in copies:
        c.wait()


def seen(mask_ref, first, key_block, query_block):
    sub = lax.broadcasted_iota(jnp.int32, key_block.shape, 0)
    blocks = mask_ref.shape[1] // 2
    table = jnp.zeros(key_block.shape, F32)
    for b in range(mask_ref.shape[0]):
        for kb in range(blocks):
            here = (sub == b) & (key_block == kb)
            table = jnp.where(here, mask_ref[b, first + kb].astype(F32), table)
    one_hot = (sub == query_block).astype(F32)
    return dot(table.astype(BF16), one_hot.astype(BF16), TN)


def forward_body(scale, q_ref, prev_ref, own_ref, next_ref, mask_ref, prob_ref, attf_ref, att_ref):
    tokens = q_ref.shape[0]
    width = own_ref.shape[1] // 2
    group = QUERY_HEADS // KEY_VALUE_HEADS
    blocks = mask_ref.shape[1] // 2
    ids = [r[tokens:, :tokens].astype(F32).astype(jnp.int32) for r in (prev_ref, own_ref, next_ref)]
    see_prev = seen(mask_ref, 0, ids[0], ids[1]) > 0.5
    see_next = seen(mask_ref, blocks, ids[2], ids[1]) > 0.5
    for g in range(KEY_VALUE_HEADS):
        cols = slice(g * HEAD_WIDTH, (g + 1) * HEAD_WIDTH)
        vcols = slice(width + g * HEAD_WIDTH, width + (g + 1) * HEAD_WIDTH)
        keys = jnp.concatenate([r[:tokens, cols] for r in (prev_ref, own_ref, next_ref)], 0)
        values = jnp.concatenate([r[:tokens, vcols] for r in (prev_ref, own_ref, next_ref)], 0)
        values_t = values.T
        for j in range(group):
            h = g * group + j
            at = slice(h * HEAD_WIDTH, (h + 1) * HEAD_WIDTH)
            scores = dot(keys, q_ref[:, at], NT) * scale
            low = jnp.where(see_prev, scores[:tokens], -1e30)
            mid = scores[tokens : 2 * tokens]
            high = jnp.where(see_next, scores[2 * tokens :], -1e30)
            top = jnp.maximum(jnp.maximum(low, mid), high).max(axis=0, keepdims=True)
            low, mid, high = jnp.exp(low - top), jnp.exp(mid - top), jnp.exp(high - top)
            inverse = 1.0 / (low + mid + high).sum(axis=0, keepdims=True)
            prob = jnp.concatenate([(low * inverse), (mid * inverse), (high * inverse)], 0).astype(BF16)
            prob_ref[:, at] = prob
            att = dot(values_t, prob, NN)
            attf_ref[at, :] = att
            att_ref[at, :] = att.astype(BF16)


def split_body(att_ref, keep_ref, send_ref):
    mine = lax.rem(lax.axis_index("dp"), 2)
    for z in range(QUERY_HEADS // 2):
        to = slice(z * HEAD_WIDTH, (z + 1) * HEAD_WIDTH)
        keep = pl.multiple_of((2 * z + mine) * HEAD_WIDTH, HEAD_WIDTH)
        send = pl.multiple_of((2 * z + 1 - mine) * HEAD_WIDTH, HEAD_WIDTH)
        keep_ref[to, :] = att_ref[pl.ds(keep, HEAD_WIDTH), :]
        send_ref[to, :] = att_ref[pl.ds(send, HEAD_WIDTH), :]


def weight_part_body(parts, keep_ref, other_ref, dy_ref, dy_other_ref, *outs):
    me = lax.axis_index("ctx")
    cols = dy_ref.shape[1] // parts
    left = jnp.concatenate([keep_ref[...], other_ref[...]], 1)
    for m, out in enumerate(outs):
        at = pl.ds(pl.multiple_of((me ^ m) * cols, cols), cols)
        right = jnp.concatenate([dy_ref[:, at], dy_other_ref[:, at]], 0)
        out[...] = dot(left, right, NN).astype(out.dtype)


def weight_plane_body(count, *refs):
    ins, outs = refs[:count], refs[count:]
    me = lax.axis_index("dp") // 2
    rows = outs[0].shape[0]
    for m, out in enumerate(outs):
        at = pl.ds(pl.multiple_of(lax.rem(me + m, len(outs)) * rows, rows), rows)
        total = ins[0][at, :].astype(F32)
        for r in ins[1:]:
            total = total + r[at, :].astype(F32)
        out[...] = total.astype(out.dtype)


def weight_sum_body(factor, *refs):
    total = refs[0][...].astype(F32)
    for r in refs[1:-1]:
        total = total + r[...].astype(F32)
    refs[-1][...] = total * factor


def head_at(h):
    start = h * HEAD_WIDTH
    return pl.ds(start if isinstance(h, int) else pl.multiple_of(start, HEAD_WIDTH), HEAD_WIDTH)


def lanes_at(start):
    return pl.ds(start if isinstance(start, int) else pl.multiple_of(start, HEAD_WIDTH), HEAD_WIDTH)


def band_of(refs, tokens, start):
    return jnp.concatenate([r[:tokens, lanes_at(start)] for r in refs], 0)


def heads_backward(heads, group, q_ref, band, dy_ref, prob_ref, attf_ref, pieces, ds_ref, first):
    tokens = q_ref.shape[0]
    width = band[0].shape[1] // 2
    values = band_of(band, tokens, width + group * HEAD_WIDTH)
    probs, d_rows, q_rows = [], [], []
    for i, (h, piece) in enumerate(zip(heads, pieces)):
        at = head_at(h)
        dat = dot(piece[...], dy_ref[...], NT).astype(BF16)
        delta = (dat.astype(F32) * attf_ref[at, :]).sum(axis=0, keepdims=True)
        prob = prob_ref[:, at]
        ds_ref[:, head_at(first + i)] = (prob.astype(F32) * (dot(values, dat, NN) - delta)).astype(BF16)
        probs.append(prob)
        d_rows.append(dat.T)
        q_rows.append(q_ref[:, at])
    ds = ds_ref[:, first * HEAD_WIDTH : (first + len(heads)) * HEAD_WIDTH]
    part_k = dot(ds, jnp.concatenate(q_rows, 0), NN)
    part_v = dot(jnp.concatenate(probs, 1), jnp.concatenate(d_rows, 0), NN)
    return part_k, part_v


def backward_first_body(scale, place, q_ref, prev_ref, own_ref, next_ref, dy_ref, prob_ref, attf_ref, *rest):
    pieces, (whole_ref, half_ref, ds_ref) = rest[:6], rest[6:]
    head, group = place()
    band = (prev_ref, own_ref, next_ref)
    shared = (q_ref, band, dy_ref, prob_ref, attf_ref)
    part_k, part_v = heads_backward([head(j) for j in range(4)], group(0), *shared, pieces[:4], ds_ref, 0)
    whole_ref[:, :HEAD_WIDTH] = (part_k * scale).astype(BF16)
    whole_ref[:, HEAD_WIDTH:] = part_v.astype(BF16)
    part_k, part_v = heads_backward([head(j) for j in (4, 5)], group(4), *shared, pieces[4:], ds_ref, 4)
    half_ref[:, :HEAD_WIDTH] = part_k
    half_ref[:, HEAD_WIDTH:] = part_v


def backward_second_body(scale, place, q_ref, prev_ref, own_ref, next_ref, dy_ref, prob_ref, attf_ref, *rest):
    pieces, whole_ref, half_ref = rest[:2], rest[2], rest[3]
    outs, ds_ref = rest[4:7], rest[7]
    head, group = place()
    tokens = q_ref.shape[0]
    width = own_ref.shape[1] // 2
    band = (prev_ref, own_ref, next_ref)
    shared = (q_ref, band, dy_ref, prob_ref, attf_ref)
    part_k, part_v = heads_backward([head(j) for j in (6, 7)], group(6), *shared, pieces, ds_ref, 0)
    part_k = ((part_k + half_ref[:, :HEAD_WIDTH]) * scale).astype(BF16)
    part_v = (part_v + half_ref[:, HEAD_WIDTH:]).astype(BF16)
    for t, out in enumerate(outs):
        rows = slice(t * tokens, (t + 1) * tokens)
        out[:, lanes_at(group(6) * HEAD_WIDTH)] = part_k[rows]
        out[:, lanes_at(width + group(6) * HEAD_WIDTH)] = part_v[rows]
        out[:, lanes_at(group(0) * HEAD_WIDTH)] = whole_ref[rows, :HEAD_WIDTH]
        out[:, lanes_at(width + group(0) * HEAD_WIDTH)] = whole_ref[rows, HEAD_WIDTH:]


def output_body(scale, place, prev_ref, own_ref, next_ref, ds_ref, ds_last_ref, att_ref, *rest):
    pieces, (mixed_ref, gq_ref) = rest[:QUERY_HEADS], rest[QUERY_HEADS:]
    head, group = place()
    tokens = mixed_ref.shape[0]
    ds = (ds_ref[:, : 4 * HEAD_WIDTH], jnp.concatenate([ds_ref[:, 4 * HEAD_WIDTH :], ds_last_ref[...]], 1))
    for half in range(2):
        keys = band_of((prev_ref, own_ref, next_ref), tokens, group(4 * half) * HEAD_WIDTH)
        dq = dot(keys.T, ds[half], NN) * scale
        for i in range(4):
            gq_ref[:, head_at(head(4 * half + i))] = dq[:, i * tokens : (i + 1) * tokens].T.astype(BF16)
    total = jnp.zeros(mixed_ref.shape, F32)
    for j in range(0, QUERY_HEADS, 2):
        att = jnp.concatenate([att_ref[head_at(head(i)), :].T for i in (j, j + 1)], 1)
        total = total + dot(att, jnp.concatenate([pieces[j][...], pieces[j + 1][...]], 0), NN)
    mixed_ref[...] = total.astype(BF16)


def key_value_body(own_ref, low_ref, high_ref, gk_ref, gv_ref):
    width = gk_ref.shape[1]
    total = own_ref[...].astype(F32) + low_ref[...].astype(F32) + high_ref[...].astype(F32)
    gk_ref[...] = total[:, :width].astype(BF16)
    gv_ref[...] = total[:, width:].astype(BF16)


def power_of_two(n):
    return n & (n - 1) == 0


def flip(value, axis, mask):
    return lax.ppermute(value, axis, [(i, i ^ mask) for i in range(lax.axis_size(axis))])


def turn(value, axis, step):
    count = lax.axis_size(axis)
    return lax.ppermute(value, axis, [(i, (i + step) % count) for i in range(count)])


def sublayer(queries, keys_in, values_in, patch_order, block_mask, out_weight, cotangent):
    scale = 1.0 / math.sqrt(HEAD_WIDTH)
    n_dp, n_ctx = lax.axis_size("dp"), lax.axis_size("ctx")
    q, k, v, dy = queries[0], keys_in[0], values_in[0], cotangent[0]
    tokens, query_width = q.shape
    kv_width = k.shape[1]
    model = dy.shape[1]
    band = 3 * tokens
    by_head = n_dp == QUERY_HEADS
    column_width = model // n_ctx
    staged = by_head and power_of_two(n_ctx) and column_width % 128 == 0
    macs = tokens * query_width
    group_heads = QUERY_HEADS // KEY_VALUE_HEADS

    own = call(
        pack_body,
        [shape((tokens + HALO_ROWS, 2 * kv_width))],
        [hbm()] * 3,
        in_hbm(k, v, patch_order[0]),
        scratch=[pltpu.VMEM((1, tokens), jnp.int32), pltpu.SemaphoreType.DMA((3,))],
        room=16<<20,
    )[0]
    dy_hbm = dy
    q, dy = call(
        fetch_body, [shape(q.shape), shape(dy.shape)], [hbm()] * 2, in_hbm(q, dy),
        scratch=[pltpu.SemaphoreType.DMA((2,))],
    )
    prev_kv = turn(own, "ctx", 1)
    next_kv = turn(own, "ctx", -1)

    if by_head:
        mine = {0: out_weight}
        for j in range(n_dp // 2, 1, -2):
            mine[j] = flip(out_weight, "dp", j)
        for j in range(n_dp // 2 + 2, n_dp, 2):
            mine[j] = flip(mine[n_dp // 2], "dp", j - n_dp // 2)

        def place():
            me = lax.axis_index("dp")
            return (lambda j: me ^ j), (lambda j: (me ^ j) // group_heads)
    else:
        weight_all = lax.all_gather(out_weight, "dp", axis=0, tiled=True)
        pieces = [weight_all.reshape(QUERY_HEADS, HEAD_WIDTH, model)[h] for h in range(QUERY_HEADS)]

        def place():
            return (lambda j: j), (lambda j: j // group_heads)

    prob, attf, att = call(
        functools.partial(forward_body, scale),
        [shape((band, query_width)), shape((query_width, tokens), F32), shape((query_width, tokens))],
        [vmem()] * 4 + [smem()],
        (q, prev_kv, own, next_kv, block_mask[0]),
        flops=4 * macs * band,
    )

    total_tokens = n_dp * tokens * n_ctx
    norm_factor = 1.0 / math.sqrt(total_tokens)
    if staged:
        dy_other = flip(dy_hbm, "dp", 1)
        half = query_width // 2
        keep, send = call(split_body, [shape((half, tokens))] * 2, [vmem()], (att,))
        other = flip(send, "dp", 1)
        parts = call(
            functools.partial(weight_part_body, n_ctx),
            [shape((half, column_width))] * n_ctx,
            [vmem()] * 4,
            (keep, other, dy, dy_other),
            flops=2 * half * 2 * tokens * model,
        )
        arrived = [parts[0]]
        for m in range(1, n_ctx):
            arrived.append(flip(parts[m], "ctx", m))
        n_z = n_dp // 2
        blocks = call(
            functools.partial(weight_plane_body, n_ctx),
            [shape((half // n_z, column_width))] * n_z,
            [vmem()] * n_ctx,
            arrived,
        )
        landed = [blocks[0]]
        for m in range(1, n_z):
            landed.append(turn(blocks[m], "dp", 2 * m))
        grad_weight = call(
            functools.partial(weight_sum_body, norm_factor),
            [shape((half // n_z, column_width), F32)],
            [vmem()] * n_z,
            landed,
        )[0]
    else:
        part = dot(att, dy, NN).astype(BF16)
        columns = lax.psum_scatter(part, "ctx", scatter_dimension=1, tiled=True).astype(F32)
        grad_weight = lax.psum_scatter(columns, "dp", scatter_dimension=0, tiled=True) * norm_factor

    if by_head:
        pieces = []
        for j in range(0, n_dp, 2):
            pieces += [mine[j], flip(mine[j], "dp", 1)]

    whole, half_sum, ds = call(
        functools.partial(backward_first_body, scale, place),
        [shape((band, 2 * HEAD_WIDTH)), shape((band, 2 * HEAD_WIDTH), F32), shape((band, 6 * HEAD_WIDTH))],
        [vmem()] * 13,
        (q, prev_kv, own, next_kv, dy, prob, attf, *pieces[:6]),
        flops=(2 * macs * model + 6 * macs * band) * 3 // 4,
    )
    low, mid, high, ds_last = call(
        functools.partial(backward_second_body, scale, place),
        [shape((tokens, 2 * kv_width))] * 3 + [shape((band, 2 * HEAD_WIDTH))],
        [vmem()] * 11,
        (q, prev_kv, own, next_kv, dy, prob, attf, *pieces[6:], whole, half_sum),
        flops=(2 * macs * model + 6 * macs * band) // 4,
    )
    from_next = turn(low, "ctx", -1)
    from_prev = turn(high, "ctx", 1)
    mixed, grad_q = call(
        functools.partial(output_body, scale, place),
        [shape((tokens, model)), shape((tokens, query_width))],
        [vmem()] * 14,
        (prev_kv, own, next_kv, ds, ds_last, att, *pieces),
        flops=2 * macs * model + 2 * macs * band,
    )
    grad_k, grad_v = call(key_value_body, [shape((tokens, kv_width))] * 2, [vmem()] * 3, (mid, from_next, from_prev))
    return (mixed[None], grad_q[None], grad_k[None], grad_v[None], grad_weight)


def solution(mesh):
    row = P("dp", "ctx", None)
    in_specs = (row, row, row, row, row, P("dp", None), row)
    out_specs = (row, row, row, row, P("dp", "ctx"))
    return jax.shard_map(sublayer, mesh=mesh, in_specs=in_specs, out_specs=out_specs, check_vma=False)
```

```python
import functools
import math

import jax
import jax.numpy as jnp
from jax import lax
from jax.experimental import pallas as pl
from jax.experimental.pallas import tpu as pltpu
from jax.sharding import PartitionSpec as P

QUERY_HEADS = 8
KEY_VALUE_HEADS = 2
HEAD_WIDTH = 128
BLK = 32
HALO_ROWS = 8


F32 = jnp.float32
BF16 = jnp.bfloat16
NN = (((1,), (0,)), ((), ()))
NT = (((1,), (1,)), ((), ()))
TN = (((0,), (0,)), ((), ()))


def dot(a, b, dims):
    return lax.dot_general(a, b, dims, preferred_element_type=F32)


def vmem():
    return pl.BlockSpec(memory_space=pltpu.VMEM)


def smem():
    return pl.BlockSpec(memory_space=pltpu.SMEM)


def hbm():
    return pl.BlockSpec(memory_space=pltpu.HBM)


def in_hbm(*arrays):
    return tuple(pltpu.with_memory_space_constraint(a, pltpu.HBM) for a in arrays)


def call(body, outs, specs, args, scratch=(), flops=1 << 20, room=16 << 20):
    moved = sum(a.size * a.dtype.itemsize for a in (*args, *outs))
    return pl.pallas_call(
        body,
        out_shape=outs,
        in_specs=specs,
        out_specs=[vmem() for _ in outs],
        scratch_shapes=list(scratch),
        cost_estimate=pl.CostEstimate(flops=flops, bytes_accessed=moved, transcendentals=0),
        compiler_params=pltpu.CompilerParams(vmem_limit_bytes=room),
    )(*args)


def shape(dims, dtype=BF16):
    return jax.ShapeDtypeStruct(dims, dtype)


def pack_body(k_ref, v_ref, order_ref, out_ref, order_scr, sem):
    tokens, width = k_ref.shape
    copies = [
        pltpu.make_async_copy(order_ref, order_scr, sem.at[0]),
        pltpu.make_async_copy(k_ref, out_ref.at[:tokens, :width], sem.at[1]),
        pltpu.make_async_copy(v_ref, out_ref.at[:tokens, width:], sem.at[2]),
    ]
    for c in copies:
        c.start()
    copies[0].wait()
    row = lax.broadcasted_iota(jnp.int32, (tokens, tokens), 0)
    holds = (row == order_scr[...]).astype(F32).astype(BF16)
    block = lax.broadcasted_iota(jnp.int32, (HALO_ROWS, tokens), 1) // BLK
    out_ref[tokens:, :] = jnp.zeros((HALO_ROWS, 2 * width), BF16)
    out_ref[tokens:, :tokens] = dot(block.astype(F32).astype(BF16), holds, NT).astype(BF16)
    copies[1].wait()
    copies[2].wait()


def fetch_body(a_ref, b_ref, a_out, b_out, sem):
    copies = [
        pltpu.make_async_copy(a_ref, a_out, sem.at[0]),
        pltpu.make_async_copy(b_ref, b_out, sem.at[1]),
    ]
    for c in copies:
        c.start()
    for c in copies:
        c.wait()


def seen(mask_ref, first, key_block, query_block):
    sub = lax.broadcasted_iota(jnp.int32, key_block.shape, 0)
    blocks = mask_ref.shape[1] // 2
    table = jnp.zeros(key_block.shape, F32)
    for b in range(mask_ref.shape[0]):
        for kb in range(blocks):
            here = (sub == b) & (key_block == kb)
            table = jnp.where(here, mask_ref[b, first + kb].astype(F32), table)
    one_hot = (sub == query_block).astype(F32)
    return dot(table.astype(BF16), one_hot.astype(BF16), TN)


def forward_body(scale, q_ref, prev_ref, own_ref, next_ref, mask_ref, prob_ref, attf_ref, att_ref):
    tokens = q_ref.shape[0]
    width = own_ref.shape[1] // 2
    group = QUERY_HEADS // KEY_VALUE_HEADS
    blocks = mask_ref.shape[1] // 2
    ids = [r[tokens:, :tokens].astype(F32).astype(jnp.int32) for r in (prev_ref, own_ref, next_ref)]
    see_prev = seen(mask_ref, 0, ids[0], ids[1]) > 0.5
    see_next = seen(mask_ref, blocks, ids[2], ids[1]) > 0.5
    for g in range(KEY_VALUE_HEADS):
        cols = slice(g * HEAD_WIDTH, (g + 1) * HEAD_WIDTH)
        vcols = slice(width + g * HEAD_WIDTH, width + (g + 1) * HEAD_WIDTH)
        keys = jnp.concatenate([r[:tokens, cols] for r in (prev_ref, own_ref, next_ref)], 0)
        values = jnp.concatenate([r[:tokens, vcols] for r in (prev_ref, own_ref, next_ref)], 0)
        values_t = values.T
        for j in range(group):
            h = g * group + j
            at = slice(h * HEAD_WIDTH, (h + 1) * HEAD_WIDTH)
            scores = dot(keys, q_ref[:, at], NT) * scale
            low = jnp.where(see_prev, scores[:tokens], -1e30)
            mid = scores[tokens : 2 * tokens]
            high = jnp.where(see_next, scores[2 * tokens :], -1e30)
            top = jnp.maximum(jnp.maximum(low, mid), high).max(axis=0, keepdims=True)
            low, mid, high = jnp.exp(low - top), jnp.exp(mid - top), jnp.exp(high - top)
            inverse = 1.0 / (low + mid + high).sum(axis=0, keepdims=True)
            prob = jnp.concatenate([(low * inverse), (mid * inverse), (high * inverse)], 0).astype(BF16)
            prob_ref[:, at] = prob
            att = dot(values_t, prob, NN)
            attf_ref[at, :] = att
            att_ref[at, :] = att.astype(BF16)


def split_body(att_ref, keep_ref, send_ref):
    mine = lax.rem(lax.axis_index("dp"), 2)
    for z in range(QUERY_HEADS // 2):
        to = slice(z * HEAD_WIDTH, (z + 1) * HEAD_WIDTH)
        keep = pl.multiple_of((2 * z + mine) * HEAD_WIDTH, HEAD_WIDTH)
        send = pl.multiple_of((2 * z + 1 - mine) * HEAD_WIDTH, HEAD_WIDTH)
        keep_ref[to, :] = att_ref[pl.ds(keep, HEAD_WIDTH), :]
        send_ref[to, :] = att_ref[pl.ds(send, HEAD_WIDTH), :]


def weight_part_body(parts, keep_ref, other_ref, dy_ref, dy_other_ref, *outs):
    me = lax.axis_index("ctx")
    cols = dy_ref.shape[1] // parts
    left = jnp.concatenate([keep_ref[...], other_ref[...]], 1)
    for m, out in enumerate(outs):
        at = pl.ds(pl.multiple_of((me ^ m) * cols, cols), cols)
        right = jnp.concatenate([dy_ref[:, at], dy_other_ref[:, at]], 0)
        out[...] = dot(left, right, NN).astype(out.dtype)


def weight_plane_body(count, *refs):
    ins, outs = refs[:count], refs[count:]
    me = lax.axis_index("dp") // 2
    rows = outs[0].shape[0]
    for m, out in enumerate(outs):
        at = pl.ds(pl.multiple_of((me ^ m) * rows, rows), rows)
        total = ins[0][at, :].astype(F32)
        for r in ins[1:]:
            total = total + r[at, :].astype(F32)
        out[...] = total.astype(out.dtype)


def weight_sum_body(factor, *refs):
    total = refs[0][...].astype(F32)
    for r in refs[1:-1]:
        total = total + r[...].astype(F32)
    refs[-1][...] = total * factor


def head_at(h):
    start = h * HEAD_WIDTH
    return pl.ds(start if isinstance(h, int) else pl.multiple_of(start, HEAD_WIDTH), HEAD_WIDTH)


def lanes_at(start):
    return pl.ds(start if isinstance(start, int) else pl.multiple_of(start, HEAD_WIDTH), HEAD_WIDTH)


def band_of(refs, tokens, start):
    return jnp.concatenate([r[:tokens, lanes_at(start)] for r in refs], 0)


def heads_backward(heads, group, q_ref, band, dy_ref, prob_ref, attf_ref, pieces, ds_ref, first):
    tokens = q_ref.shape[0]
    width = band[0].shape[1] // 2
    values = band_of(band, tokens, width + group * HEAD_WIDTH)
    probs, d_rows, q_rows = [], [], []
    for i, (h, piece) in enumerate(zip(heads, pieces)):
        at = head_at(h)
        dat = dot(piece[...], dy_ref[...], NT).astype(BF16)
        delta = (dat.astype(F32) * attf_ref[at, :]).sum(axis=0, keepdims=True)
        prob = prob_ref[:, at]
        ds_ref[:, head_at(first + i)] = (prob.astype(F32) * (dot(values, dat, NN) - delta)).astype(BF16)
        probs.append(prob)
        d_rows.append(dat.T)
        q_rows.append(q_ref[:, at])
    ds = ds_ref[:, first * HEAD_WIDTH : (first + len(heads)) * HEAD_WIDTH]
    part_k = dot(ds, jnp.concatenate(q_rows, 0), NN)
    part_v = dot(jnp.concatenate(probs, 1), jnp.concatenate(d_rows, 0), NN)
    return part_k, part_v


def backward_first_body(scale, place, q_ref, prev_ref, own_ref, next_ref, dy_ref, prob_ref, attf_ref, *rest):
    pieces, (whole_ref, half_ref, ds_ref) = rest[:6], rest[6:]
    head, group = place()
    band = (prev_ref, own_ref, next_ref)
    shared = (q_ref, band, dy_ref, prob_ref, attf_ref)
    part_k, part_v = heads_backward([head(j) for j in range(4)], group(0), *shared, pieces[:4], ds_ref, 0)
    whole_ref[:, :HEAD_WIDTH] = (part_k * scale).astype(BF16)
    whole_ref[:, HEAD_WIDTH:] = part_v.astype(BF16)
    part_k, part_v = heads_backward([head(j) for j in (4, 5)], group(4), *shared, pieces[4:], ds_ref, 4)
    half_ref[:, :HEAD_WIDTH] = part_k
    half_ref[:, HEAD_WIDTH:] = part_v


def backward_second_body(place, q_ref, prev_ref, own_ref, next_ref, dy_ref, prob_ref, attf_ref, *rest):
    piece, half_ref, more_ref, ds_ref = rest
    head, group = place()
    shared = (q_ref, (prev_ref, own_ref, next_ref), dy_ref, prob_ref, attf_ref)
    part_k, part_v = heads_backward([head(6)], group(6), *shared, [piece], ds_ref, 0)
    more_ref[:, :HEAD_WIDTH] = part_k + half_ref[:, :HEAD_WIDTH]
    more_ref[:, HEAD_WIDTH:] = part_v + half_ref[:, HEAD_WIDTH:]


def backward_third_body(scale, place, q_ref, prev_ref, own_ref, next_ref, dy_ref, prob_ref, attf_ref, *rest):
    piece, whole_ref, half_ref = rest[:3]
    outs, ds_ref = rest[3:6], rest[6]
    head, group = place()
    tokens = q_ref.shape[0]
    width = own_ref.shape[1] // 2
    band = (prev_ref, own_ref, next_ref)
    shared = (q_ref, band, dy_ref, prob_ref, attf_ref)
    part_k, part_v = heads_backward([head(7)], group(6), *shared, [piece], ds_ref, 0)
    part_k = ((part_k + half_ref[:, :HEAD_WIDTH]) * scale).astype(BF16)
    part_v = (part_v + half_ref[:, HEAD_WIDTH:]).astype(BF16)
    for t, out in enumerate(outs):
        rows = slice(t * tokens, (t + 1) * tokens)
        out[:, lanes_at(group(6) * HEAD_WIDTH)] = part_k[rows]
        out[:, lanes_at(width + group(6) * HEAD_WIDTH)] = part_v[rows]
        out[:, lanes_at(group(0) * HEAD_WIDTH)] = whole_ref[rows, :HEAD_WIDTH]
        out[:, lanes_at(width + group(0) * HEAD_WIDTH)] = whole_ref[rows, HEAD_WIDTH:]


def output_body(scale, place, prev_ref, own_ref, next_ref, ds_ref, ds_more_ref, ds_last_ref, att_ref, *rest):
    pieces, (mixed_ref, gq_ref) = rest[:QUERY_HEADS], rest[QUERY_HEADS:]
    head, group = place()
    tokens = mixed_ref.shape[0]
    ds = (ds_ref[:, : 4 * HEAD_WIDTH], jnp.concatenate([ds_ref[:, 4 * HEAD_WIDTH :], ds_more_ref[...], ds_last_ref[...]], 1))
    for half in range(2):
        keys = band_of((prev_ref, own_ref, next_ref), tokens, group(4 * half) * HEAD_WIDTH)
        dq = dot(keys.T, ds[half], NN) * scale
        for i in range(4):
            gq_ref[:, head_at(head(4 * half + i))] = dq[:, i * tokens : (i + 1) * tokens].T.astype(BF16)
    total = jnp.zeros(mixed_ref.shape, F32)
    for j in range(0, QUERY_HEADS, 2):
        att = jnp.concatenate([att_ref[head_at(head(i)), :].T for i in (j, j + 1)], 1)
        total = total + dot(att, jnp.concatenate([pieces[j][...], pieces[j + 1][...]], 0), NN)
    mixed_ref[...] = total.astype(BF16)


def key_value_body(own_ref, low_ref, high_ref, gk_ref, gv_ref):
    width = gk_ref.shape[1]
    total = own_ref[...].astype(F32) + low_ref[...].astype(F32) + high_ref[...].astype(F32)
    gk_ref[...] = total[:, :width].astype(BF16)
    gv_ref[...] = total[:, width:].astype(BF16)


def power_of_two(n):
    return n & (n - 1) == 0


def flip(value, axis, mask):
    return lax.ppermute(value, axis, [(i, i ^ mask) for i in range(lax.axis_size(axis))])


def turn(value, axis, step):
    count = lax.axis_size(axis)
    return lax.ppermute(value, axis, [(i, (i + step) % count) for i in range(count)])


def sublayer(queries, keys_in, values_in, patch_order, block_mask, out_weight, cotangent):
    scale = 1.0 / math.sqrt(HEAD_WIDTH)
    n_dp, n_ctx = lax.axis_size("dp"), lax.axis_size("ctx")
    q, k, v, dy = queries[0], keys_in[0], values_in[0], cotangent[0]
    tokens, query_width = q.shape
    kv_width = k.shape[1]
    model = dy.shape[1]
    band = 3 * tokens
    by_head = n_dp == QUERY_HEADS
    column_width = model // n_ctx
    staged = by_head and power_of_two(n_ctx) and column_width % 128 == 0
    macs = tokens * query_width
    group_heads = QUERY_HEADS // KEY_VALUE_HEADS

    own = call(
        pack_body,
        [shape((tokens + HALO_ROWS, 2 * kv_width))],
        [hbm()] * 3,
        in_hbm(k, v, patch_order[0]),
        scratch=[pltpu.VMEM((1, tokens), jnp.int32), pltpu.SemaphoreType.DMA((3,))],
        room=16<<20,
    )[0]
    dy_hbm = dy
    q, dy = call(
        fetch_body, [shape(q.shape), shape(dy.shape)], [hbm()] * 2, in_hbm(q, dy),
        scratch=[pltpu.SemaphoreType.DMA((2,))],
    )
    prev_kv = turn(own, "ctx", 1)
    next_kv = turn(own, "ctx", -1)

    if by_head:
        mine = {0: out_weight}
        for j in range(n_dp // 2, 1, -2):
            mine[j] = flip(out_weight, "dp", j)
        for j in range(n_dp // 2 + 2, n_dp, 2):
            mine[j] = flip(mine[n_dp // 2], "dp", j - n_dp // 2)

        def place():
            me = lax.axis_index("dp")
            return (lambda j: me ^ j), (lambda j: (me ^ j) // group_heads)
    else:
        weight_all = lax.all_gather(out_weight, "dp", axis=0, tiled=True)
        pieces = [weight_all.reshape(QUERY_HEADS, HEAD_WIDTH, model)[h] for h in range(QUERY_HEADS)]

        def place():
            return (lambda j: j), (lambda j: j // group_heads)

    prob, attf, att = call(
        functools.partial(forward_body, scale),
        [shape((band, query_width)), shape((query_width, tokens), F32), shape((query_width, tokens))],
        [vmem()] * 4 + [smem()],
        (q, prev_kv, own, next_kv, block_mask[0]),
        flops=4 * macs * band,
    )

    total_tokens = n_dp * tokens * n_ctx
    norm_factor = 1.0 / math.sqrt(total_tokens)
    if staged:
        dy_other = flip(dy_hbm, "dp", 1)
        half = query_width // 2
        keep, send = call(split_body, [shape((half, tokens))] * 2, [vmem()], (att,))
        other = flip(send, "dp", 1)
        parts = call(
            functools.partial(weight_part_body, n_ctx),
            [shape((half, column_width))] * n_ctx,
            [vmem()] * 4,
            (keep, other, dy, dy_other),
            flops=2 * half * 2 * tokens * model,
        )
        arrived = [parts[0]]
        for m in range(1, n_ctx):
            arrived.append(flip(parts[m], "ctx", m))
        n_z = n_dp // 2
        blocks = call(
            functools.partial(weight_plane_body, n_ctx),
            [shape((half // n_z, column_width))] * n_z,
            [vmem()] * n_ctx,
            arrived,
        )
        landed = [blocks[0]]
        for m in range(1, n_z):
            landed.append(flip(blocks[m], "dp", 2 * m))
        grad_weight = call(
            functools.partial(weight_sum_body, norm_factor),
            [shape((half // n_z, column_width), F32)],
            [vmem()] * n_z,
            landed,
        )[0]
    else:
        part = dot(att, dy, NN).astype(BF16)
        columns = lax.psum_scatter(part, "ctx", scatter_dimension=1, tiled=True).astype(F32)
        grad_weight = lax.psum_scatter(columns, "dp", scatter_dimension=0, tiled=True) * norm_factor

    if by_head:
        pieces = []
        for j in range(0, n_dp, 2):
            pieces += [mine[j], flip(mine[j], "dp", 1)]

    whole, half_sum, ds = call(
        functools.partial(backward_first_body, scale, place),
        [shape((band, 2 * HEAD_WIDTH)), shape((band, 2 * HEAD_WIDTH), F32), shape((band, 6 * HEAD_WIDTH))],
        [vmem()] * 13,
        (q, prev_kv, own, next_kv, dy, prob, attf, *pieces[:6]),
        flops=(2 * macs * model + 6 * macs * band) * 3 // 4,
    )
    shared = (q, prev_kv, own, next_kv, dy, prob, attf)
    one_head = (2 * macs * model + 6 * macs * band) // QUERY_HEADS
    half_sum, ds_more = call(
        functools.partial(backward_second_body, place),
        [shape((band, 2 * HEAD_WIDTH), F32), shape((band, HEAD_WIDTH))],
        [vmem()] * 9,
        (*shared, pieces[6], half_sum),
        flops=one_head,
    )
    low, mid, high, ds_last = call(
        functools.partial(backward_third_body, scale, place),
        [shape((tokens, 2 * kv_width))] * 3 + [shape((band, HEAD_WIDTH))],
        [vmem()] * 10,
        (*shared, pieces[7], whole, half_sum),
        flops=one_head,
    )
    from_next = turn(low, "ctx", -1)
    from_prev = turn(high, "ctx", 1)
    mixed, grad_q = call(
        functools.partial(output_body, scale, place),
        [shape((tokens, model)), shape((tokens, query_width))],
        [vmem()] * 15,
        (prev_kv, own, next_kv, ds, ds_more, ds_last, att, *pieces),
        flops=2 * macs * model + 2 * macs * band,
    )
    grad_k, grad_v = call(key_value_body, [shape((tokens, kv_width))] * 2, [vmem()] * 3, (mid, from_next, from_prev))
    return (mixed[None], grad_q[None], grad_k[None], grad_v[None], grad_weight)


def solution(mesh):
    row = P("dp", "ctx", None)
    in_specs = (row, row, row, row, row, P("dp", None), row)
    out_specs = (row, row, row, row, P("dp", "ctx"))
    return jax.shard_map(sublayer, mesh=mesh, in_specs=in_specs, out_specs=out_specs, check_vma=False)
```

```python
import functools
import math

import jax
import jax.numpy as jnp
from jax import lax
from jax.experimental import pallas as pl
from jax.experimental.pallas import tpu as pltpu
from jax.sharding import PartitionSpec as P

QUERY_HEADS = 8
KEY_VALUE_HEADS = 2
HEAD_WIDTH = 128
BLK = 32
PAIRS = QUERY_HEADS // 2
HALO_ROWS = 8


F32 = jnp.float32
BF16 = jnp.bfloat16
NN = (((1,), (0,)), ((), ()))
NT = (((1,), (1,)), ((), ()))
TN = (((0,), (0,)), ((), ()))


def dot(a, b, dims):
    return lax.dot_general(a, b, dims, preferred_element_type=F32)


def vmem():
    return pl.BlockSpec(memory_space=pltpu.VMEM)


def hbm():
    return pl.BlockSpec(memory_space=pltpu.HBM)


def in_hbm(*arrays):
    return tuple(pltpu.with_memory_space_constraint(a, pltpu.HBM) for a in arrays)


def call(body, outs, specs, args, scratch=(), flops=1 << 20, room=16 << 20):
    moved = sum(a.size * a.dtype.itemsize for a in (*args, *outs))
    return pl.pallas_call(
        body,
        out_shape=outs,
        in_specs=specs,
        out_specs=[vmem() for _ in outs],
        scratch_shapes=list(scratch),
        cost_estimate=pl.CostEstimate(flops=flops, bytes_accessed=moved, transcendentals=0),
        compiler_params=pltpu.CompilerParams(vmem_limit_bytes=room),
    )(*args)


def shape(dims, dtype=BF16):
    return jax.ShapeDtypeStruct(dims, dtype)


def pack_body(k_ref, v_ref, order_ref, out_ref, order_scr, sem):
    tokens, width = k_ref.shape
    copies = [
        pltpu.make_async_copy(order_ref, order_scr, sem.at[0]),
        pltpu.make_async_copy(k_ref, out_ref.at[:tokens, :width], sem.at[1]),
        pltpu.make_async_copy(v_ref, out_ref.at[:tokens, width:], sem.at[2]),
    ]
    for c in copies:
        c.start()
    copies[0].wait()
    row = lax.broadcasted_iota(jnp.int32, (tokens, tokens), 0)
    holds = (row == order_scr[...]).astype(F32).astype(BF16)
    block = lax.broadcasted_iota(jnp.int32, (HALO_ROWS, tokens), 1) // BLK
    out_ref[tokens:, :] = jnp.zeros((HALO_ROWS, 2 * width), BF16)
    out_ref[tokens:, :tokens] = dot(block.astype(F32).astype(BF16), holds, NT).astype(BF16)
    copies[1].wait()
    copies[2].wait()


def fetch_body(a_ref, b_ref, mask_ref, a_out, b_out, table_out, mask_scr, sem):
    copies = [
        pltpu.make_async_copy(mask_ref, mask_scr, sem.at[0]),
        pltpu.make_async_copy(a_ref, a_out, sem.at[1]),
        pltpu.make_async_copy(b_ref, b_out, sem.at[2]),
    ]
    for c in copies:
        c.start()
    copies[0].wait()
    rows, columns = mask_ref.shape
    sub = lax.broadcasted_iota(jnp.int32, (HALO_ROWS, table_out.shape[1]), 0)
    for kb in range(columns):
        spread = jnp.zeros(sub.shape, F32)
        for b in range(rows):
            spread = jnp.where(sub == b, mask_scr[b, kb].astype(F32), spread)
        table_out[kb * HALO_ROWS : (kb + 1) * HALO_ROWS, :] = spread
    copies[1].wait()
    copies[2].wait()


def seen(table_ref, first, blocks, key_block, query_block):
    sub = lax.broadcasted_iota(jnp.int32, key_block.shape, 0)
    table = jnp.zeros(key_block.shape, F32)
    for kb in range(blocks):
        at = (first + kb) * HALO_ROWS
        table = jnp.where(key_block == kb, table_ref[at : at + HALO_ROWS, :], table)
    one_hot = (sub == query_block).astype(F32)
    return dot(table.astype(BF16), one_hot.astype(BF16), TN)


def forward_body(scale, place, side, q_ref, prev_ref, own_ref, next_ref, table_ref, prob_ref, attf_ref, att_ref):
    head, _ = place()
    tokens = q_ref.shape[0]
    width = own_ref.shape[1] // 2
    blocks = table_ref.shape[0] // HALO_ROWS // 2
    ids = [r[tokens:, :tokens].astype(F32).astype(jnp.int32) for r in (prev_ref, own_ref, next_ref)]
    see_prev = seen(table_ref, 0, blocks, ids[0], ids[1]) > 0.5
    see_next = seen(table_ref, blocks, blocks, ids[2], ids[1]) > 0.5
    band = (prev_ref, own_ref, next_ref)
    for g in range(KEY_VALUE_HEADS):
        keys = band_of(band, tokens, g * HEAD_WIDTH)
        values_t = band_of(band, tokens, width + g * HEAD_WIDTH).T
        for pair in range(g * PAIRS // KEY_VALUE_HEADS, (g + 1) * PAIRS // KEY_VALUE_HEADS):
            at = head_at(pair)
            scores = dot(keys, q_ref[:, head_at(2 * pair + lax.rem(head(side), 2))], NT) * scale
            low = jnp.where(see_prev, scores[:tokens], -1e30)
            mid = scores[tokens : 2 * tokens]
            high = jnp.where(see_next, scores[2 * tokens :], -1e30)
            top = jnp.maximum(jnp.maximum(low, mid), high).max(axis=0, keepdims=True)
            low, mid, high = jnp.exp(low - top), jnp.exp(mid - top), jnp.exp(high - top)
            inverse = 1.0 / (low + mid + high).sum(axis=0, keepdims=True)
            prob = jnp.concatenate([low * inverse, mid * inverse, high * inverse], 0).astype(BF16)
            prob_ref[:, at] = prob
            att = dot(values_t, prob, NN)
            attf_ref[at, :] = att
            att_ref[at, :] = att.astype(BF16)


def weight_part_body(parts, keep_ref, other_ref, dy_ref, dy_other_ref, *outs):
    me = lax.axis_index("ctx")
    cols = dy_ref.shape[1] // parts
    left = jnp.concatenate([keep_ref[...], other_ref[...]], 1)
    for m, out in enumerate(outs):
        at = pl.ds(pl.multiple_of((me ^ m) * cols, cols), cols)
        right = jnp.concatenate([dy_ref[:, at], dy_other_ref[:, at]], 0)
        out[...] = dot(left, right, NN).astype(out.dtype)


def weight_plane_body(count, *refs):
    ins, outs = refs[:count], refs[count:]
    me = lax.axis_index("dp") // 2
    rows = outs[0].shape[0]
    for m, out in enumerate(outs):
        at = pl.ds(pl.multiple_of((me ^ m) * rows, rows), rows)
        total = ins[0][at, :].astype(F32)
        for r in ins[1:]:
            total = total + r[at, :].astype(F32)
        out[...] = total.astype(out.dtype)


def weight_sum_body(factor, *refs):
    total = refs[0][...].astype(F32)
    for r in refs[1:-1]:
        total = total + r[...].astype(F32)
    refs[-1][...] = total * factor


def head_at(h):
    start = h * HEAD_WIDTH
    return pl.ds(start if isinstance(h, int) else pl.multiple_of(start, HEAD_WIDTH), HEAD_WIDTH)


def lanes_at(start):
    return pl.ds(start if isinstance(start, int) else pl.multiple_of(start, HEAD_WIDTH), HEAD_WIDTH)


def band_of(refs, tokens, start):
    return jnp.concatenate([r[:tokens, lanes_at(start)] for r in refs], 0)


def heads_backward(place, js, q_ref, band, dy_ref, probs, attfs, pieces, ds_ref, first):
    head, group = place()
    tokens = q_ref.shape[0]
    width = band[0].shape[1] // 2
    values = band_of(band, tokens, width + group(js[0]) * HEAD_WIDTH)
    prob_list, d_rows, q_rows = [], [], []
    for i, (j, piece) in enumerate(zip(js, pieces)):
        at = head_at(head(j) // 2)
        dat = dot(piece[...], dy_ref[...], NT).astype(BF16)
        delta = (dat.astype(F32) * attfs[j % 2][at, :]).sum(axis=0, keepdims=True)
        prob = probs[j % 2][:, at]
        ds_ref[:, head_at(first + i)] = (prob.astype(F32) * (dot(values, dat, NN) - delta)).astype(BF16)
        prob_list.append(prob)
        d_rows.append(dat.T)
        q_rows.append(q_ref[:, head_at(head(j))])
    ds = ds_ref[:, first * HEAD_WIDTH : (first + len(js)) * HEAD_WIDTH]
    part_k = dot(ds, jnp.concatenate(q_rows, 0), NN)
    part_v = dot(jnp.concatenate(prob_list, 1), jnp.concatenate(d_rows, 0), NN)
    return part_k, part_v


def backward_first_body(scale, place, q_ref, prev_ref, own_ref, next_ref, dy_ref, p0, p1, a0, a1, *rest):
    pieces, (whole_ref, half_ref, ds_ref) = rest[:6], rest[6:]
    shared = (q_ref, (prev_ref, own_ref, next_ref), dy_ref, (p0, p1), (a0, a1))
    part_k, part_v = heads_backward(place, range(4), *shared, pieces[:4], ds_ref, 0)
    whole_ref[:, :HEAD_WIDTH] = (part_k * scale).astype(BF16)
    whole_ref[:, HEAD_WIDTH:] = part_v.astype(BF16)
    part_k, part_v = heads_backward(place, (4, 5), *shared, pieces[4:], ds_ref, 4)
    half_ref[:, :HEAD_WIDTH] = part_k
    half_ref[:, HEAD_WIDTH:] = part_v


def backward_second_body(scale, place, q_ref, prev_ref, own_ref, next_ref, dy_ref, p0, p1, a0, a1, *rest):
    pieces, whole_ref, half_ref = rest[:2], rest[2], rest[3]
    outs, ds_ref = rest[4:7], rest[7]
    _, group = place()
    tokens = q_ref.shape[0]
    width = own_ref.shape[1] // 2
    shared = (q_ref, (prev_ref, own_ref, next_ref), dy_ref, (p0, p1), (a0, a1))
    part_k, part_v = heads_backward(place, (6, 7), *shared, pieces, ds_ref, 0)
    part_k = ((part_k + half_ref[:, :HEAD_WIDTH]) * scale).astype(BF16)
    part_v = (part_v + half_ref[:, HEAD_WIDTH:]).astype(BF16)
    for t, out in enumerate(outs):
        rows = slice(t * tokens, (t + 1) * tokens)
        out[:, lanes_at(group(6) * HEAD_WIDTH)] = part_k[rows]
        out[:, lanes_at(width + group(6) * HEAD_WIDTH)] = part_v[rows]
        out[:, lanes_at(group(0) * HEAD_WIDTH)] = whole_ref[rows, :HEAD_WIDTH]
        out[:, lanes_at(width + group(0) * HEAD_WIDTH)] = whole_ref[rows, HEAD_WIDTH:]


def output_body(scale, place, prev_ref, own_ref, next_ref, ds_ref, ds_last_ref, t0, t1, *rest):
    pieces, (mixed_ref, gq_ref) = rest[:QUERY_HEADS], rest[QUERY_HEADS:]
    head, group = place()
    tokens = mixed_ref.shape[0]
    ds = (ds_ref[:, : 4 * HEAD_WIDTH], jnp.concatenate([ds_ref[:, 4 * HEAD_WIDTH :], ds_last_ref[...]], 1))
    for half in range(2):
        keys = band_of((prev_ref, own_ref, next_ref), tokens, group(4 * half) * HEAD_WIDTH)
        dq = dot(keys.T, ds[half], NN) * scale
        for i in range(4):
            gq_ref[:, head_at(head(4 * half + i))] = dq[:, i * tokens : (i + 1) * tokens].T.astype(BF16)
    total = jnp.zeros(mixed_ref.shape, F32)
    for j in range(0, QUERY_HEADS, 2):
        at = head_at(head(j) // 2)
        att = jnp.concatenate([t0[at, :].T, t1[at, :].T], 1)
        total = total + dot(att, jnp.concatenate([pieces[j][...], pieces[j + 1][...]], 0), NN)
    mixed_ref[...] = total.astype(BF16)


def key_value_body(own_ref, low_ref, high_ref, gk_ref, gv_ref):
    width = gk_ref.shape[1]
    total = own_ref[...].astype(F32) + low_ref[...].astype(F32) + high_ref[...].astype(F32)
    gk_ref[...] = total[:, :width].astype(BF16)
    gv_ref[...] = total[:, width:].astype(BF16)


def power_of_two(n):
    return n & (n - 1) == 0


def flip(value, axis, mask):
    return lax.ppermute(value, axis, [(i, i ^ mask) for i in range(lax.axis_size(axis))])


def turn(value, axis, step):
    count = lax.axis_size(axis)
    return lax.ppermute(value, axis, [(i, (i + step) % count) for i in range(count)])


def sublayer(queries, keys_in, values_in, patch_order, block_mask, out_weight, cotangent):
    scale = 1.0 / math.sqrt(HEAD_WIDTH)
    n_dp, n_ctx = lax.axis_size("dp"), lax.axis_size("ctx")
    q, k, v, dy = queries[0], keys_in[0], values_in[0], cotangent[0]
    tokens, query_width = q.shape
    kv_width = k.shape[1]
    model = dy.shape[1]
    band = 3 * tokens
    by_head = n_dp == QUERY_HEADS
    column_width = model // n_ctx
    staged = by_head and power_of_two(n_ctx) and column_width % 128 == 0
    macs = tokens * query_width
    group_heads = QUERY_HEADS // KEY_VALUE_HEADS

    own = call(
        pack_body,
        [shape((tokens + HALO_ROWS, 2 * kv_width))],
        [hbm()] * 3,
        in_hbm(k, v, patch_order[0]),
        scratch=[pltpu.VMEM((1, tokens), jnp.int32), pltpu.SemaphoreType.DMA((3,))],
        room=16<<20,
    )[0]
    dy_hbm = dy
    mask = block_mask[0]
    q, dy, table = call(
        fetch_body,
        [shape(q.shape), shape(dy.shape), shape((mask.shape[1] * HALO_ROWS, tokens), F32)],
        [hbm()] * 3,
        in_hbm(q, dy, mask),
        scratch=[pltpu.SMEM(mask.shape, jnp.int32), pltpu.SemaphoreType.DMA((3,))],
    )
    prev_kv = turn(own, "ctx", 1)
    next_kv = turn(own, "ctx", -1)

    if by_head:
        mine = {0: out_weight}
        for j in range(n_dp // 2, 1, -2):
            mine[j] = flip(out_weight, "dp", j)
        for j in range(n_dp // 2 + 2, n_dp, 2):
            mine[j] = flip(mine[n_dp // 2], "dp", j - n_dp // 2)

        def place():
            me = lax.axis_index("dp")
            return (lambda j: me ^ j), (lambda j: (me ^ j) // group_heads)
    else:
        weight_all = lax.all_gather(out_weight, "dp", axis=0, tiled=True)
        pieces = [weight_all.reshape(QUERY_HEADS, HEAD_WIDTH, model)[h] for h in range(QUERY_HEADS)]

        def place():
            return (lambda j: j), (lambda j: j // group_heads)

    half = query_width // 2
    prob, attf, att = [], [], []
    for side in (1, 0):
        done = call(
            functools.partial(forward_body, scale, place, side),
            [shape((band, half)), shape((half, tokens), F32), shape((half, tokens))],
            [vmem()] * 5,
            (q, prev_kv, own, next_kv, table),
            flops=2 * macs * band,
        )
        for held, new in zip((prob, attf, att), done):
            held.insert(0, new)

    total_tokens = n_dp * tokens * n_ctx
    norm_factor = 1.0 / math.sqrt(total_tokens)
    if staged:
        dy_other = flip(dy_hbm, "dp", 1)
        other = flip(att[1], "dp", 1)
        parts = call(
            functools.partial(weight_part_body, n_ctx),
            [shape((half, column_width))] * n_ctx,
            [vmem()] * 4,
            (att[0], other, dy, dy_other),
            flops=2 * half * 2 * tokens * model,
        )
        arrived = [parts[0]]
        for m in range(1, n_ctx):
            arrived.append(flip(parts[m], "ctx", m))
        n_z = n_dp // 2
        blocks = call(
            functools.partial(weight_plane_body, n_ctx),
            [shape((half // n_z, column_width))] * n_z,
            [vmem()] * n_ctx,
            arrived,
        )
        landed = [blocks[0]]
        for m in range(1, n_z):
            landed.append(flip(blocks[m], "dp", 2 * m))
        grad_weight = call(
            functools.partial(weight_sum_body, norm_factor),
            [shape((half // n_z, column_width), F32)],
            [vmem()] * n_z,
            landed,
        )[0]
    else:
        by_pair = jnp.stack([a.reshape(PAIRS, HEAD_WIDTH, tokens) for a in att], 1)
        part = dot(by_pair.reshape(query_width, tokens), dy, NN).astype(BF16)
        columns = lax.psum_scatter(part, "ctx", scatter_dimension=1, tiled=True).astype(F32)
        grad_weight = lax.psum_scatter(columns, "dp", scatter_dimension=0, tiled=True) * norm_factor

    if by_head:
        pieces = []
        for j in range(0, n_dp, 2):
            pieces += [mine[j], flip(mine[j], "dp", 1)]

    whole, half_sum, ds = call(
        functools.partial(backward_first_body, scale, place),
        [shape((band, 2 * HEAD_WIDTH)), shape((band, 2 * HEAD_WIDTH), F32), shape((band, 6 * HEAD_WIDTH))],
        [vmem()] * 15,
        (q, prev_kv, own, next_kv, dy, *prob, *attf, *pieces[:6]),
        flops=(2 * macs * model + 6 * macs * band) * 3 // 4,
    )
    low, mid, high, ds_last = call(
        functools.partial(backward_second_body, scale, place),
        [shape((tokens, 2 * kv_width))] * 3 + [shape((band, 2 * HEAD_WIDTH))],
        [vmem()] * 13,
        (q, prev_kv, own, next_kv, dy, *prob, *attf, *pieces[6:], whole, half_sum),
        flops=(2 * macs * model + 6 * macs * band) // 4,
    )
    from_next = turn(low, "ctx", -1)
    from_prev = turn(high, "ctx", 1)
    mixed, grad_q = call(
        functools.partial(output_body, scale, place),
        [shape((tokens, model)), shape((tokens, query_width))],
        [vmem()] * 15,
        (prev_kv, own, next_kv, ds, ds_last, *att, *pieces),
        flops=2 * macs * model + 2 * macs * band,
    )
    grad_k, grad_v = call(key_value_body, [shape((tokens, kv_width))] * 2, [vmem()] * 3, (mid, from_next, from_prev))
    return (mixed[None], grad_q[None], grad_k[None], grad_v[None], grad_weight)


def solution(mesh):
    row = P("dp", "ctx", None)
    in_specs = (row, row, row, row, row, P("dp", None), row)
    out_specs = (row, row, row, row, P("dp", "ctx"))
    return jax.shard_map(sublayer, mesh=mesh, in_specs=in_specs, out_specs=out_specs, check_vma=False)
```

```python
import functools
import math

import jax
import jax.numpy as jnp
from jax import lax
from jax.experimental import pallas as pl
from jax.experimental.pallas import tpu as pltpu
from jax.sharding import PartitionSpec as P

QUERY_HEADS = 8
KEY_VALUE_HEADS = 2
HEAD_WIDTH = 128
BLK = 32
PAIRS = QUERY_HEADS // 2
HALO_ROWS = 8


F32 = jnp.float32
BF16 = jnp.bfloat16
NN = (((1,), (0,)), ((), ()))
NT = (((1,), (1,)), ((), ()))
TN = (((0,), (0,)), ((), ()))


def dot(a, b, dims):
    return lax.dot_general(a, b, dims, preferred_element_type=F32)


def vmem():
    return pl.BlockSpec(memory_space=pltpu.VMEM)


def hbm():
    return pl.BlockSpec(memory_space=pltpu.HBM)


def in_hbm(*arrays):
    return tuple(pltpu.with_memory_space_constraint(a, pltpu.HBM) for a in arrays)


def call(body, outs, specs, args, scratch=(), flops=1 << 20, room=16 << 20):
    moved = sum(a.size * a.dtype.itemsize for a in (*args, *outs))
    return pl.pallas_call(
        body,
        out_shape=outs,
        in_specs=specs,
        out_specs=[vmem() for _ in outs],
        scratch_shapes=list(scratch),
        cost_estimate=pl.CostEstimate(flops=flops, bytes_accessed=moved, transcendentals=0),
        compiler_params=pltpu.CompilerParams(vmem_limit_bytes=room),
    )(*args)


def shape(dims, dtype=BF16):
    return jax.ShapeDtypeStruct(dims, dtype)


def pack_body(k_ref, v_ref, order_ref, out_ref, order_scr, sem):
    tokens, width = k_ref.shape
    copies = [
        pltpu.make_async_copy(order_ref, order_scr, sem.at[0]),
        pltpu.make_async_copy(k_ref, out_ref.at[:tokens, :width], sem.at[1]),
        pltpu.make_async_copy(v_ref, out_ref.at[:tokens, width:], sem.at[2]),
    ]
    for c in copies:
        c.start()
    copies[0].wait()
    row = lax.broadcasted_iota(jnp.int32, (tokens, tokens), 0)
    holds = (row == order_scr[...]).astype(F32).astype(BF16)
    block = lax.broadcasted_iota(jnp.int32, (HALO_ROWS, tokens), 1) // BLK
    out_ref[tokens:, :] = jnp.zeros((HALO_ROWS, 2 * width), BF16)
    out_ref[tokens:, :tokens] = dot(block.astype(F32).astype(BF16), holds, NT).astype(BF16)
    copies[1].wait()
    copies[2].wait()


def fetch_body(a_ref, b_ref, mask_ref, a_out, b_out, table_out, mask_scr, sem):
    copies = [
        pltpu.make_async_copy(mask_ref, mask_scr, sem.at[0]),
        pltpu.make_async_copy(a_ref, a_out, sem.at[1]),
        pltpu.make_async_copy(b_ref, b_out, sem.at[2]),
    ]
    for c in copies:
        c.start()
    copies[0].wait()
    rows, columns = mask_ref.shape
    sub = lax.broadcasted_iota(jnp.int32, (HALO_ROWS, table_out.shape[1]), 0)
    for kb in range(columns):
        spread = jnp.zeros(sub.shape, F32)
        for b in range(rows):
            spread = jnp.where(sub == b, mask_scr[b, kb].astype(F32), spread)
        table_out[kb * HALO_ROWS : (kb + 1) * HALO_ROWS, :] = spread
    copies[1].wait()
    copies[2].wait()


def seen(table_ref, first, blocks, key_block, query_block):
    sub = lax.broadcasted_iota(jnp.int32, key_block.shape, 0)
    table = jnp.zeros(key_block.shape, F32)
    for kb in range(blocks):
        at = (first + kb) * HALO_ROWS
        table = jnp.where(key_block == kb, table_ref[at : at + HALO_ROWS, :], table)
    one_hot = (sub == query_block).astype(F32)
    return dot(table.astype(BF16), one_hot.astype(BF16), TN)


def forward_body(scale, place, side, q_ref, prev_ref, own_ref, next_ref, table_ref, prob_ref, attf_ref, att_ref):
    head, _ = place()
    tokens = q_ref.shape[0]
    width = own_ref.shape[1] // 2
    blocks = table_ref.shape[0] // HALO_ROWS // 2
    ids = [r[tokens:, :tokens].astype(F32).astype(jnp.int32) for r in (prev_ref, own_ref, next_ref)]
    see_prev = seen(table_ref, 0, blocks, ids[0], ids[1]) > 0.5
    see_next = seen(table_ref, blocks, blocks, ids[2], ids[1]) > 0.5
    band = (prev_ref, own_ref, next_ref)
    for g in range(KEY_VALUE_HEADS):
        keys = band_of(band, tokens, g * HEAD_WIDTH)
        values_t = band_of(band, tokens, width + g * HEAD_WIDTH).T
        for pair in range(g * PAIRS // KEY_VALUE_HEADS, (g + 1) * PAIRS // KEY_VALUE_HEADS):
            at = head_at(pair)
            scores = dot(keys, q_ref[:, head_at(2 * pair + lax.rem(head(side), 2))], NT) * scale
            low = jnp.where(see_prev, scores[:tokens], -1e30)
            mid = scores[tokens : 2 * tokens]
            high = jnp.where(see_next, scores[2 * tokens :], -1e30)
            top = jnp.maximum(jnp.maximum(low, mid), high).max(axis=0, keepdims=True)
            low, mid, high = jnp.exp(low - top), jnp.exp(mid - top), jnp.exp(high - top)
            inverse = 1.0 / (low + mid + high).sum(axis=0, keepdims=True)
            prob = jnp.concatenate([low * inverse, mid * inverse, high * inverse], 0).astype(BF16)
            prob_ref[:, at] = prob
            att = dot(values_t, prob, NN)
            attf_ref[at, :] = att
            att_ref[at, :] = att.astype(BF16)


def weight_part_body(parts, keep_ref, other_ref, dy_ref, dy_other_ref, *outs):
    me = lax.axis_index("ctx")
    cols = dy_ref.shape[1] // parts
    left = jnp.concatenate([keep_ref[...], other_ref[...]], 1)
    for m, out in enumerate(outs):
        at = pl.ds(pl.multiple_of((me ^ m) * cols, cols), cols)
        right = jnp.concatenate([dy_ref[:, at], dy_other_ref[:, at]], 0)
        out[...] = dot(left, right, NN).astype(out.dtype)


def weight_plane_body(count, *refs):
    ins, outs = refs[:count], refs[count:]
    me = lax.axis_index("dp") // 2
    rows = outs[0].shape[0]
    for m, out in enumerate(outs):
        at = pl.ds(pl.multiple_of((me ^ m) * rows, rows), rows)
        total = ins[0][at, :].astype(F32)
        for r in ins[1:]:
            total = total + r[at, :].astype(F32)
        out[...] = total.astype(out.dtype)


def weight_sum_body(factor, *refs):
    total = refs[0][...].astype(F32)
    for r in refs[1:-1]:
        total = total + r[...].astype(F32)
    refs[-1][...] = total * factor


def head_at(h):
    start = h * HEAD_WIDTH
    return pl.ds(start if isinstance(h, int) else pl.multiple_of(start, HEAD_WIDTH), HEAD_WIDTH)


def lanes_at(start):
    return pl.ds(start if isinstance(start, int) else pl.multiple_of(start, HEAD_WIDTH), HEAD_WIDTH)


def band_of(refs, tokens, start):
    return jnp.concatenate([r[:tokens, lanes_at(start)] for r in refs], 0)


def heads_backward(place, js, q_ref, band, dy_ref, probs, attfs, pieces, ds_ref, first):
    head, group = place()
    tokens = q_ref.shape[0]
    width = band[0].shape[1] // 2
    values = band_of(band, tokens, width + group(js[0]) * HEAD_WIDTH)
    prob_list, d_rows, q_rows = [], [], []
    for i, (j, piece) in enumerate(zip(js, pieces)):
        at = head_at(head(j) // 2)
        dat = dot(piece[...], dy_ref[...], NT).astype(BF16)
        delta = (dat.astype(F32) * attfs[j % 2][at, :]).sum(axis=0, keepdims=True)
        prob = probs[j % 2][:, at]
        ds_ref[:, head_at(first + i)] = (prob.astype(F32) * (dot(values, dat, NN) - delta)).astype(BF16)
        prob_list.append(prob)
        d_rows.append(dat.T)
        q_rows.append(q_ref[:, head_at(head(j))])
    ds = ds_ref[:, first * HEAD_WIDTH : (first + len(js)) * HEAD_WIDTH]
    part_k = dot(ds, jnp.concatenate(q_rows, 0), NN)
    part_v = dot(jnp.concatenate(prob_list, 1), jnp.concatenate(d_rows, 0), NN)
    return part_k, part_v


def backward_first_body(scale, place, q_ref, prev_ref, own_ref, next_ref, dy_ref, p0, p1, a0, a1, *rest):
    pieces, (whole_ref, half_ref, ds_ref) = rest[:6], rest[6:]
    shared = (q_ref, (prev_ref, own_ref, next_ref), dy_ref, (p0, p1), (a0, a1))
    part_k, part_v = heads_backward(place, range(4), *shared, pieces[:4], ds_ref, 0)
    whole_ref[:, :HEAD_WIDTH] = (part_k * scale).astype(BF16)
    whole_ref[:, HEAD_WIDTH:] = part_v.astype(BF16)
    part_k, part_v = heads_backward(place, (4, 5), *shared, pieces[4:], ds_ref, 4)
    half_ref[:, :HEAD_WIDTH] = part_k
    half_ref[:, HEAD_WIDTH:] = part_v


def backward_second_body(scale, place, q_ref, prev_ref, own_ref, next_ref, dy_ref, p0, p1, a0, a1, *rest):
    pieces, whole_ref, half_ref = rest[:2], rest[2], rest[3]
    outs, ds_ref = rest[4:7], rest[7]
    _, group = place()
    tokens = q_ref.shape[0]
    width = own_ref.shape[1] // 2
    shared = (q_ref, (prev_ref, own_ref, next_ref), dy_ref, (p0, p1), (a0, a1))
    part_k, part_v = heads_backward(place, (6, 7), *shared, pieces, ds_ref, 0)
    part_k = ((part_k + half_ref[:, :HEAD_WIDTH]) * scale).astype(BF16)
    part_v = (part_v + half_ref[:, HEAD_WIDTH:]).astype(BF16)
    for t, out in enumerate(outs):
        rows = slice(t * tokens, (t + 1) * tokens)
        out[:, lanes_at(group(6) * HEAD_WIDTH)] = part_k[rows]
        out[:, lanes_at(width + group(6) * HEAD_WIDTH)] = part_v[rows]
        out[:, lanes_at(group(0) * HEAD_WIDTH)] = whole_ref[rows, :HEAD_WIDTH]
        out[:, lanes_at(width + group(0) * HEAD_WIDTH)] = whole_ref[rows, HEAD_WIDTH:]


def output_body(scale, place, prev_ref, own_ref, next_ref, ds_ref, ds_last_ref, t0, t1, *rest):
    pieces, (mixed_ref, gq_ref) = rest[:QUERY_HEADS], rest[QUERY_HEADS:]
    head, group = place()
    tokens = mixed_ref.shape[0]
    ds = (ds_ref[:, : 4 * HEAD_WIDTH], jnp.concatenate([ds_ref[:, 4 * HEAD_WIDTH :], ds_last_ref[...]], 1))
    for half in range(2):
        keys = band_of((prev_ref, own_ref, next_ref), tokens, group(4 * half) * HEAD_WIDTH)
        dq = dot(keys.T, ds[half], NN) * scale
        for i in range(4):
            gq_ref[:, head_at(head(4 * half + i))] = dq[:, i * tokens : (i + 1) * tokens].T.astype(BF16)
    total = jnp.zeros(mixed_ref.shape, F32)
    for j in range(0, QUERY_HEADS, 2):
        at = head_at(head(j) // 2)
        att = jnp.concatenate([t0[at, :].T, t1[at, :].T], 1)
        total = total + dot(att, jnp.concatenate([pieces[j][...], pieces[j + 1][...]], 0), NN)
    mixed_ref[...] = total.astype(BF16)


def key_value_body(own_ref, low_ref, high_ref, gk_ref, gv_ref):
    width = gk_ref.shape[1]
    total = own_ref[...].astype(F32) + low_ref[...].astype(F32) + high_ref[...].astype(F32)
    gk_ref[...] = total[:, :width].astype(BF16)
    gv_ref[...] = total[:, width:].astype(BF16)


def power_of_two(n):
    return n & (n - 1) == 0


def flip(value, axis, mask):
    return lax.ppermute(value, axis, [(i, i ^ mask) for i in range(lax.axis_size(axis))])


def turn(value, axis, step):
    count = lax.axis_size(axis)
    return lax.ppermute(value, axis, [(i, (i + step) % count) for i in range(count)])


def sublayer(queries, keys_in, values_in, patch_order, block_mask, out_weight, cotangent):
    scale = 1.0 / math.sqrt(HEAD_WIDTH)
    n_dp, n_ctx = lax.axis_size("dp"), lax.axis_size("ctx")
    q, k, v, dy = queries[0], keys_in[0], values_in[0], cotangent[0]
    tokens, query_width = q.shape
    kv_width = k.shape[1]
    model = dy.shape[1]
    band = 3 * tokens
    column_width = model // n_ctx
    by_head = n_dp == QUERY_HEADS and power_of_two(n_ctx) and column_width % 128 == 0
    macs = tokens * query_width
    group_heads = QUERY_HEADS // KEY_VALUE_HEADS

    own = call(
        pack_body,
        [shape((tokens + HALO_ROWS, 2 * kv_width))],
        [hbm()] * 3,
        in_hbm(k, v, patch_order[0]),
        scratch=[pltpu.VMEM((1, tokens), jnp.int32), pltpu.SemaphoreType.DMA((3,))],
        room=16<<20,
    )[0]
    dy_hbm = dy
    mask = block_mask[0]
    q, dy, table = call(
        fetch_body,
        [shape(q.shape), shape(dy.shape), shape((mask.shape[1] * HALO_ROWS, tokens), F32)],
        [hbm()] * 3,
        in_hbm(q, dy, mask),
        scratch=[pltpu.SMEM(mask.shape, jnp.int32), pltpu.SemaphoreType.DMA((3,))],
    )
    prev_kv = turn(own, "ctx", 1)
    next_kv = turn(own, "ctx", -1)

    if by_head:
        mine = {0: out_weight}
        for j in range(n_dp // 2, 1, -2):
            mine[j] = flip(out_weight, "dp", j)
        for j in range(n_dp // 2 + 2, n_dp, 2):
            mine[j] = flip(mine[n_dp // 2], "dp", j - n_dp // 2)

        def place():
            me = lax.axis_index("dp")
            return (lambda j: me ^ j), (lambda j: (me ^ j) // group_heads)
    else:
        weight_all = lax.all_gather(out_weight, "dp", axis=0, tiled=True)
        pieces = [weight_all.reshape(QUERY_HEADS, HEAD_WIDTH, model)[h] for h in range(QUERY_HEADS)]

        def place():
            return (lambda j: j), (lambda j: j // group_heads)

    half = query_width // 2
    prob, attf, att = [], [], []
    for side in (1, 0):
        done = call(
            functools.partial(forward_body, scale, place, side),
            [shape((band, half)), shape((half, tokens), F32), shape((half, tokens))],
            [vmem()] * 5,
            (q, prev_kv, own, next_kv, table),
            flops=2 * macs * band,
        )
        for held, new in zip((prob, attf, att), done):
            held.insert(0, new)

    total_tokens = n_dp * tokens * n_ctx
    norm_factor = 1.0 / math.sqrt(total_tokens)
    if by_head:
        dy_other = flip(dy_hbm, "dp", 1)
        other = flip(att[1], "dp", 1)
        parts = call(
            functools.partial(weight_part_body, n_ctx),
            [shape((half, column_width))] * n_ctx,
            [vmem()] * 4,
            (att[0], other, dy, dy_other),
            flops=2 * half * 2 * tokens * model,
        )
        arrived = [parts[0]]
        for m in range(1, n_ctx):
            arrived.append(flip(parts[m], "ctx", m))
        n_z = n_dp // 2
        blocks = call(
            functools.partial(weight_plane_body, n_ctx),
            [shape((half // n_z, column_width))] * n_z,
            [vmem()] * n_ctx,
            arrived,
        )
        landed = [blocks[0]]
        for m in range(1, n_z):
            landed.append(flip(blocks[m], "dp", 2 * m))
        grad_weight = call(
            functools.partial(weight_sum_body, norm_factor),
            [shape((half // n_z, column_width), F32)],
            [vmem()] * n_z,
            landed,
        )[0]
    else:
        by_pair = jnp.stack([a.reshape(PAIRS, HEAD_WIDTH, tokens) for a in att], 1)
        part = dot(by_pair.reshape(query_width, tokens), dy, NN).astype(BF16)
        columns = lax.psum_scatter(part, "ctx", scatter_dimension=1, tiled=True).astype(F32)
        grad_weight = lax.psum_scatter(columns, "dp", scatter_dimension=0, tiled=True) * norm_factor

    if by_head:
        pieces = []
        for j in range(0, n_dp, 2):
            pieces += [mine[j], flip(mine[j], "dp", 1)]

    whole, half_sum, ds = call(
        functools.partial(backward_first_body, scale, place),
        [shape((band, 2 * HEAD_WIDTH)), shape((band, 2 * HEAD_WIDTH), F32), shape((band, 6 * HEAD_WIDTH))],
        [vmem()] * 15,
        (q, prev_kv, own, next_kv, dy, *prob, *attf, *pieces[:6]),
        flops=(2 * macs * model + 6 * macs * band) * 3 // 4,
    )
    low, mid, high, ds_last = call(
        functools.partial(backward_second_body, scale, place),
        [shape((tokens, 2 * kv_width))] * 3 + [shape((band, 2 * HEAD_WIDTH))],
        [vmem()] * 13,
        (q, prev_kv, own, next_kv, dy, *prob, *attf, *pieces[6:], whole, half_sum),
        flops=(2 * macs * model + 6 * macs * band) // 4,
    )
    from_next = turn(low, "ctx", -1)
    from_prev = turn(high, "ctx", 1)
    mixed, grad_q = call(
        functools.partial(output_body, scale, place),
        [shape((tokens, model)), shape((tokens, query_width))],
        [vmem()] * 15,
        (prev_kv, own, next_kv, ds, ds_last, *att, *pieces),
        flops=2 * macs * model + 2 * macs * band,
    )
    grad_k, grad_v = call(key_value_body, [shape((tokens, kv_width))] * 2, [vmem()] * 3, (mid, from_next, from_prev))
    return (mixed[None], grad_q[None], grad_k[None], grad_v[None], grad_weight)


def solution(mesh):
    row = P("dp", "ctx", None)
    in_specs = (row, row, row, row, row, P("dp", None), row)
    out_specs = (row, row, row, row, P("dp", "ctx"))
    return jax.shard_map(sublayer, mesh=mesh, in_specs=in_specs, out_specs=out_specs, check_vma=False)
```
